128 devices in a mesh: seg: 32 (over x, y, core), cell: 4 (over z).
Axes of the slice: x: 4, y: 4, z: 4, core: 2. Of those that a mesh axis runs over, the one named last changes fastest.
Arguments:
- positions: float32 [512, 3, 512], P(('seg', 'cell')), may hold values from -6 to 6
- rest_shape: float32 [512, 3, 512], P(('seg', 'cell')), may hold values from -6 to 6
- modulus: float32 [512], P(('seg', 'cell')), may hold values from 0.5 to 2
- stiffness: bfloat16 [512, 512], replicated, may hold values from -0.25 to 0.25
- wall_points: float32 [512, 3, 512], P(('seg', 'cell')), may hold values from -6 to 6
- density: float32 [512, 3, 512], P(('seg', 'cell')), may hold values from -6 to 6
- wall_operator: float32 [512, 512], replicated, may hold values from -0.25 to 0.25
- seg_count: int32 [32], P('seg'), may hold values from 1 to 16, as said below
- neighbours: int32 [512, 4], P(('seg', 'cell')), may hold values from 0 to 511, as said below
- near_patches: int32 [512, 2], P(('seg', 'cell')), may hold values from 0 to 511, as said below
Outputs:
- new_positions: float32 [512, 3, 512], P(('seg', 'cell'))
- velocity: float32 [512, 3, 512], P(('seg', 'cell'))
- new_density: float32 [512, 3, 512], P(('seg', 'cell'))
The draws below stay inside these ranges and needn't reach their ends.
Inputs may be any that keep to these rules, and one draw needn't show every extreme that they name: `seg_count`: live cells of a segment take its slots 0 to count - 1; some segment has 16 live cells and some other has 1. `neighbours`: the first entry of cell c is c itself; every other entry is a live cell of the same segment or of a segment next to it. `near_patches`: every entry is a patch of the cell's own segment or of a segment next to it.
All inputs are finite; a program needn't handle non-finite values.
Results may differ from the reference program's by a relative error of at most 0.0037.
Values sent between devices are 32-bit elements; how exact they have to be, the bound alone decides.
A program may use at most 64 MiB of HBM per device.

```python
import math
import jax
import jax.numpy as jnp
from jax import lax

P_SIZE = 512
Q = 512
NB = 4
NW = 2
STEPS = 2
SEGMENTS = 32
SEG_CELLS = 16
SEG_PATCH = 16
CELLS = 512
PATCHES = 512


def segment_counts(key):
    base_key = jax.random.fold_in(key, 11)
    counts = jax.random.randint(jax.random.fold_in(base_key, 1), (SEGMENTS,), 1, SEG_CELLS + 1)
    fullest = jax.random.randint(jax.random.fold_in(base_key, 2), (), 0, SEGMENTS)
    emptiest = (fullest + 1 + jax.random.randint(jax.random.fold_in(base_key, 3), (), 0, SEGMENTS - 1)) % SEGMENTS
    counts = counts.at[fullest].set(SEG_CELLS).at[emptiest].set(1)
    return counts.astype(jnp.int32)


def draw_seg_count(key, part):
    return segment_counts(key)


def draw_neighbours(key, part):
    counts = segment_counts(key)
    cell_numbers = jnp.arange(CELLS, dtype=jnp.int32)
    home_segment = cell_numbers // SEG_CELLS
    stepped = jax.random.randint(jax.random.fold_in(key, 21), (CELLS, NB - 1), -1, 2)
    target = jnp.clip(home_segment[:, None] + stepped, 0, SEGMENTS - 1)
    random_bits = jax.random.randint(jax.random.fold_in(key, 22), (CELLS, NB - 1), 0, 1 << 20)
    slot_index = random_bits % counts[target]
    others = target * SEG_CELLS + slot_index
    return jnp.concatenate([cell_numbers[:, None], others], axis=1).astype(jnp.int32)


def draw_near_patches(key, part):
    cell_numbers = jnp.arange(CELLS, dtype=jnp.int32)
    home_segment = cell_numbers // SEG_CELLS
    stepped = jax.random.randint(jax.random.fold_in(key, 31), (CELLS, NW), -1, 2)
    target = jnp.clip(home_segment[:, None] + stepped, 0, SEGMENTS - 1)
    random_bits = jax.random.randint(jax.random.fold_in(key, 32), (CELLS, NW), 0, 1 << 20)
    return (target * SEG_PATCH + random_bits % SEG_PATCH).astype(jnp.int32)


def block_scale(key, extent, cuts, smallest, high):
    factor_of, own = 1.0, jax.random.fold_in(key, 6)
    for position, blocks in cuts:
        steps = jnp.exp(jax.random.uniform(jax.random.fold_in(own, position), (blocks,), jnp.float32, smallest / len(cuts), high / len(cuts)))
        factor_of = factor_of * jnp.repeat(steps, extent[position] // blocks).reshape([-1 if axis == position else 1 for axis in range(len(extent))])
    return factor_of


def gaussian(key, shape, deviation, limit, shards=(), kind=jnp.bfloat16):
    values = deviation * jax.random.normal(key, shape, jnp.float32)
    if shards:
        values = values * block_scale(key, shape, shards, -0.22, 0.18)
    return jnp.clip(values, -limit, limit).astype(kind)


def setup_inputs(seed: int = 0) -> dict:
    seeds = jax.random.split(jax.random.key(seed), 11)
    positions = gaussian(seeds[0], (CELLS, 3, P_SIZE), 1.0, 6.0, ((0, 128),), jnp.float32)
    rest_shape = gaussian(seeds[1], (CELLS, 3, P_SIZE), 1.0, 6.0, ((0, 128),), jnp.float32)
    modulus = jnp.clip(jnp.exp(math.log(2.0) - 1.3862944 * jax.random.uniform(seeds[2], (CELLS,), jnp.float32) ** block_scale(seeds[2], (CELLS,), ((0, 128),), -0.2, 0.2)), 0.5, 2.0)
    stiffness = gaussian(seeds[3], (P_SIZE, P_SIZE), P_SIZE ** -0.5, 0.25)
    wall_points = gaussian(seeds[4], (PATCHES, 3, Q), 1.0, 6.0, ((0, 128),), jnp.float32)
    density = gaussian(seeds[5], (PATCHES, 3, Q), 1.0, 6.0, ((0, 128),), jnp.float32)
    wall_operator = gaussian(seeds[6], (Q, Q), Q ** -0.5, 0.25, (), jnp.float32)
    seg_count = draw_seg_count(jax.random.fold_in(seeds[10], 71), 0)
    neighbours = draw_neighbours(jax.random.fold_in(seeds[10], 71), 0)
    near_patches = draw_near_patches(jax.random.fold_in(seeds[10], 71), 0)
    return dict(positions=positions, rest_shape=rest_shape, modulus=modulus, stiffness=stiffness, wall_points=wall_points, density=density, wall_operator=wall_operator, seg_count=seg_count, neighbours=neighbours, near_patches=near_patches)


soften_square = 0.25
stokes_factor = 0.039788735772973836
relax_factor = 0.5
time_step = 0.5
highest = lax.Precision.HIGHEST

def stokeslet(targets, sources, strength):
    apart_one = targets[0][:, None] - sources[0][None, :]
    apart_two = targets[1][:, None] - sources[1][None, :]
    apart_three = targets[2][:, None] - sources[2][None, :]
    inverse = lax.rsqrt(apart_one * apart_one + apart_two * apart_two + apart_three * apart_three + soften_square)
    along_force = apart_one * strength[0][None, :] + apart_two * strength[1][None, :] + apart_three * strength[2][None, :]
    weight = along_force * inverse * inverse * inverse
    direct = jnp.dot(inverse, strength.T, precision=highest)
    moment = jnp.dot(weight, sources.T, precision=highest)
    totals = lax.optimization_barrier(jnp.sum(weight, axis=1))
    return stokes_factor * (direct.T + targets * totals[None, :] - moment.T)

def reference(positions, rest_shape, modulus, stiffness, wall_points, density, wall_operator, seg_count, neighbours, near_patches):
    cell_numbers = jnp.arange(CELLS, dtype=jnp.int32)
    slot_index = cell_numbers % SEG_CELLS
    owner_segment = cell_numbers // SEG_CELLS
    living = (slot_index < seg_count[owner_segment]).astype(jnp.float32)
    stiff_float = stiffness.astype(jnp.float32)
    velocity = jnp.zeros_like(positions)
    for repeat in range(STEPS):
        offset = lax.optimization_barrier((positions - rest_shape).astype(jnp.bfloat16)).astype(jnp.float32)
        pushed = jnp.einsum('ckj,pj->ckp', offset, stiff_float, precision=highest)
        forces = (living * modulus)[:, None, None] * pushed

        def cell_terms(target):
            summed = jnp.zeros((3, P_SIZE), jnp.float32)
            for listed in range(NB):
                source = neighbours[target, listed]
                summed = summed + stokeslet(positions[target], positions[source], forces[source])
            pieces = []
            for listed in range(NW):
                patch_index = near_patches[target, listed]
                summed = summed + stokeslet(positions[target], wall_points[patch_index], density[patch_index])
                pieces.append(stokeslet(wall_points[patch_index], positions[target], forces[target]))
            return (summed, jnp.stack(pieces))
        moving, pieces = lax.map(cell_terms, cell_numbers)
        wall_velocity = jax.ops.segment_sum(pieces.reshape(CELLS * NW, 3, Q), near_patches.reshape(-1), num_segments=PATCHES)
        layered = jnp.einsum('pkj,ij->pki', density, wall_operator, precision=highest)
        density = density - relax_factor * (wall_velocity + 0.5 * density + layered)
        velocity = living[:, None, None] * moving
        positions = positions + time_step * velocity
    return (positions, velocity, density)
```

```python
import functools

import jax
import jax.numpy as jnp
from jax import lax
from jax.experimental import pallas as pl
from jax.experimental.pallas import tpu as pltpu
from jax.sharding import PartitionSpec as P

N = 512
OWN = 4
NZ = 4
NB = 4
NW = 2
STEPS = 2
SLOTS = 3 * NZ
PAIRS = OWN * NW
ROWS = 40

soften_square = 0.25
stokes_factor = 0.039788735772973836
relax_factor = 0.5
time_step = 0.5

f32, bf16 = jnp.float32, jnp.bfloat16
MESH = pl.DeviceIdType.MESH


def split3(v):
    a = v.astype(bf16).astype(f32)
    r = v - a
    b = r.astype(bf16).astype(f32)
    return a, b, r - b


def rows8(rows):
    index = lax.broadcasted_iota(jnp.int32, (8, N), 0)
    out = jnp.zeros((8, N), f32)
    for k, row in enumerate(rows):
        out = jnp.where(index == k, jnp.broadcast_to(row, (8, N)), out)
    return out


def dot3(a, b):
    return a[0] * b[0] + a[1] * b[1] + a[2] * b[2]


def source_factor(y):
    p = dot3(y, y)
    a, b, c = split3(rows8([-2.0 * y[0], -2.0 * y[1], -2.0 * y[2], jnp.ones_like(p), p]))
    return jnp.concatenate([a, a, b, a, b, c], 0).astype(bf16)


def target_factor(x):
    q = dot3(x, x) + soften_square
    a, b, c = split3(rows8([x[0], x[1], x[2], q, jnp.ones_like(q)]))
    return jnp.concatenate([a, b, a, c, b, a], 0).astype(bf16)


def moments(y, f):
    p, g = dot3(y, y), dot3(y, f)
    one = rows8([f[0], f[1], f[2], g] + [p * f[k] + g * y[k] for k in range(3)] + [f[0] * y[0]])
    two = rows8([f[l] * y[k] for l in range(3) for k in range(3)][1:])
    a, b, c = split3(jnp.concatenate([one, two], 0))
    return jnp.concatenate([a, b, c], 0).astype(bf16)


def fold(sums):
    return sums[0:16] + sums[16:32] + sums[32:48]


def combine(sums, x):
    row = [sums[k : k + 1] for k in range(16)]
    q = dot3(x, x) + soften_square
    m, g, h = row[0:3], row[3], row[4:7]
    t = [row[7 + 3 * l : 10 + 3 * l] for l in range(3)]
    along = dot3(x, m) - g
    return [
        stokes_factor
        * (
            q * m[k]
            - 2.0 * dot3(x, t[k])
            + h[k]
            + x[k] * along
            - (x[0] * t[0][k] + x[1] * t[1][k] + x[2] * t[2][k])
        )
        for k in range(3)
    ]


def kernel_tile(squares):
    inverse = lax.rsqrt(jnp.maximum(squares, soften_square))
    return (inverse * inverse * inverse).astype(bf16)


def mm(a, b):
    return jnp.dot(a, b, preferred_element_type=f32)


def mt(a, b):
    return lax.dot_general(a, b, (((1,), (1,)), ((), ())), preferred_element_type=f32)


def fused(
    nseg,
    pos_in,
    rest_in,
    modulus,
    stiffness,
    points_in,
    density_in,
    operator,
    seg_count,
    neighbours,
    near,
    pos_out,
    vel_out,
    den_out,
    msg_first,
    msg_second,
    wall,
    xsend,
    xrecv,
    pmat,
    pbuf,
    gcell,
    bcell,
    acc,
    pos,
    rest,
    force,
    den,
    vel,
    pieces,
    onehot,
    op1,
    op2,
    msg_send,
    msg_recv,
    wall_send,
    wall_recv,
    x_send,
    x_recv,
):
    seg = lax.axis_index("seg")
    z = lax.axis_index("cell")
    odd = seg % 2
    partner = seg + 1 - 2 * odd
    across = (seg + 2 * odd - 1 + nseg) % nseg
    own = NZ + z

    def turned(d):
        return (z + d) % NZ

    peers = []
    for step in (0, 1, -1):
        for d in range(NZ):
            if step or d:
                peers.append((step, d))

    barrier = pltpu.get_barrier_semaphore()
    for step, d in peers:
        pl.semaphore_signal(
            barrier, inc=1, device_id=((seg + step + nseg) % nseg, turned(d)), device_id_type=MESH
        )

    for ref in (pos, rest, force, den, vel):
        ref[...] = jnp.zeros_like(ref)
    wall[own] = jnp.zeros((16, N), f32)
    for c in range(OWN):
        for k in range(3):
            r = 3 * c + k
            pos[pl.ds(r, 1), :] = pos_in[c, pl.ds(k, 1), :]
            rest[pl.ds(r, 1), :] = rest_in[c, pl.ds(k, 1), :]
            den[pl.ds(r, 1), :] = density_in[c, pl.ds(k, 1), :]
            wall[own, pl.ds(r, 1), :] = points_in[c, pl.ds(k, 1), :]

    row16 = lax.broadcasted_iota(jnp.int32, (16, N), 0)
    item16 = lax.shift_right_logical(row16 * 43, 7)
    alive = jnp.zeros((16, N), f32)
    scale = jnp.zeros((16, N), f32)
    for c in range(OWN):
        one = jnp.where(z * OWN + c < seg_count[0], 1.0, 0.0).astype(f32)
        alive = jnp.where(item16 == c, one, alive)
        scale = jnp.where(item16 == c, one * modulus[c], scale)

    def send(buffer, source, target, device, send_sem, recv_sem):
        return pltpu.make_async_remote_copy(
            src_ref=buffer.at[source],
            dst_ref=buffer.at[target],
            send_sem=send_sem,
            recv_sem=recv_sem,
            device_id=device,
            device_id_type=MESH,
        )

    def start_own(copy):
        for k, d in enumerate((1, 3, 2)):
            copy(own, own, (seg, turned(d)), k).start()
        copy(own, 8 * odd + z, (partner, z), 3).start()
        copy(own, 8 - 8 * odd + z, (across, z), 4).start()

    def hand_on(copy, which):
        for k, d in which:
            slot = NZ + turned(d)
            copy(slot, slot, (seg, turned(d)), 0).wait_recv()
            copy(slot, 8 - 8 * odd + turned(d), (across, z), 5 + 2 * k).start()
            copy(slot, 8 * odd + turned(d), (partner, z), 6 + 2 * k).start()

    def wait_sides(copy):
        for d in range(NZ):
            for base in (0, 8):
                slot = base + turned(d)
                copy(slot, slot, (partner, z), 0).wait_recv()

    def wait_sent(copy):
        for k in range(11):
            copy(own, own, (partner, z), k).wait_send()

    def wall_copy(source, target, device, k):
        return send(wall, source, target, device, wall_send.at[k], wall_recv.at[target])

    first = (seg - 1) * OWN * NZ

    pl.semaphore_wait(barrier, len(peers))
    start_own(wall_copy)

    def cut(i, _):
        at = pl.ds(pl.multiple_of(i * 64, 64), 64)
        whole = operator[at, :]
        high = whole.astype(bf16)
        op1[at, :] = high
        op2[at, :] = (whole - high.astype(f32)).astype(bf16)
        return 0

    lax.fori_loop(0, N // 64, cut, 0)

    hot_row = lax.broadcasted_iota(jnp.int32, (16, 128), 0)
    hot_col = lax.broadcasted_iota(jnp.int32, (16, 128), 1)
    row_item = lax.shift_right_logical(hot_row * 43, 7)
    row_part = hot_row - 3 * row_item
    col = hot_col - jnp.where(hot_col >= 24, 24, 0) - jnp.where(hot_col >= 48, 24, 0)
    col_pair = lax.shift_right_logical(col * 43, 7)
    col_part = col - 3 * col_pair
    wanted = jnp.full((16, 128), -1, jnp.int32)
    for c in range(OWN):
        for w in range(NW):
            wanted = jnp.where(col_pair == c * NW + w, near[c, w] - first, wanted)
    fits = (row_part == col_part) & (row_item < OWN) & (hot_col < 72)
    for g in range(SLOTS):
        hit = fits & (row_item + g * OWN == wanted)
        onehot[pl.ds(g * 16, 16), :] = jnp.where(hit, 1.0, 0.0).astype(bf16)

    def rows_of(ref, base):
        return [ref[pl.ds(base + k, 1), :] for k in range(3)]

    def tiles(source, target, store):
        for k in range(4):
            store(k, kernel_tile(mm(source[k * 128 : (k + 1) * 128], target)))

    def near_rows(c, w):
        relative = jnp.clip(near[c, w] - first, 0, SLOTS * OWN - 1)
        slot, item = lax.shift_right_logical(relative, 2), lax.bitwise_and(relative, 3)
        return slot, 3 * item

    def one_step(step, msg):
        def msg_copy(source, target, device, k):
            return send(
                msg, source, target, device, msg_send.at[step, k], msg_recv.at[step, target]
            )

        offset = (pos[...] - rest[...]).astype(bf16)
        force[...] = mt(offset, stiffness[...]) * scale
        msg[own, 0:12, :] = pos[0:12, :]
        msg[own, 12:24, :] = force[0:12, :]
        msg[own, 24:36, :] = den[0:12, :]
        msg[own, 36:40, :] = jnp.zeros((4, N), f32)
        start_own(msg_copy)

        for c in range(OWN):
            x, f = rows_of(pos, 3 * c), rows_of(force, 3 * c)
            g, b = moments(x, f), target_factor(x)
            gcell[c] = g
            bcell[c] = b
            slot = c % 2

            def keep(k, value):
                pbuf[slot, pl.ds(k * 128, 128), :] = value

            tiles(source_factor(x).T, b, keep)
            acc[c] = fold(mm(g, pbuf[slot]))

        if step == 0:
            hand_on(wall_copy, ((0, 1), (1, 3), (2, 2)))
            wait_sides(wall_copy)

        hand_on(msg_copy, ((0, 1), (1, 3)))

        def reverse(c, _):
            for w in range(NW):
                slot, base = near_rows(c, w)
                y = [wall[slot, pl.ds(base + k, 1), :] for k in range(3)]
                pair = c * NW + w

                def keep(k, value):
                    pmat[pair, pl.ds(k * 128, 128), :] = value

                tiles(source_factor(y).T, bcell[c], keep)
                out = combine(fold(mt(gcell[c], pmat[pair])), y)
                for k in range(3):
                    pieces[pl.ds(3 * pair + k, 1), :] = out[k]
            return 0

        lax.fori_loop(0, OWN, reverse, 0)
        hand_on(msg_copy, ((2, 2),))

        high, middle, low = split3(pieces[...])
        spread = jnp.concatenate([high, middle, low, jnp.zeros((56, N), f32)], 0).astype(bf16)
        shares = mm(onehot[...], spread)
        for g in range(SLOTS):
            xsend[step, g] = shares[g * 16 : (g + 1) * 16]

        def x_copy(group, target, device, k):
            return pltpu.make_async_remote_copy(
                src_ref=xsend.at[step, group],
                dst_ref=xrecv.at[step, target],
                send_sem=x_send.at[step, k],
                recv_sem=x_recv.at[step, target],
                device_id=device,
                device_id_type=MESH,
            )

        for k, (away, d) in enumerate(peers):
            x_copy(
                (away + 1) * NZ + turned(d),
                (1 - away) * NZ + z,
                ((seg + away + nseg) % nseg, turned(d)),
                k,
            ).start()

        high, middle, low = split3(den[...])
        layered = fold(mt(jnp.concatenate([high, middle, low], 0).astype(bf16), op1[...]))
        second = mt(jnp.concatenate([high, middle], 0).astype(bf16), op2[...])
        layered = layered + second[0:16] + second[16:32]

        wait_sides(msg_copy)

        def forward(c, _):
            total = acc[c]
            sums = None
            for w in range(NW):
                slot, base = near_rows(c, w)
                y = [wall[slot, pl.ds(base + k, 1), :] for k in range(3)]
                f = [msg[slot, pl.ds(24 + base + k, 1), :] for k in range(3)]
                part = mm(moments(y, f), pmat[c * NW + w])
                sums = part if sums is None else sums + part
            b = bcell[c]
            for n in range(1, NB):
                relative = jnp.clip(neighbours[c, n] - first, 0, SLOTS * OWN - 1)
                slot = lax.shift_right_logical(relative, 2)
                base = 3 * lax.bitwise_and(relative, 3)
                y = [msg[slot, pl.ds(base + k, 1), :] for k in range(3)]
                f = [msg[slot, pl.ds(12 + base + k, 1), :] for k in range(3)]

                def keep(k, value):
                    pbuf[n % 2, pl.ds(k * 128, 128), :] = value

                tiles(source_factor(y).T, b, keep)
                sums = sums + mm(moments(y, f), pbuf[n % 2])
            total = total + fold(sums)
            x = rows_of(pos, 3 * c)
            out = combine(total, x)
            for k in range(3):
                vel[pl.ds(3 * c + k, 1), :] = out[k]
            return 0

        lax.fori_loop(0, OWN, forward, 0)
        speed = alive * vel[...]
        vel[...] = speed
        pos[...] = pos[...] + time_step * speed

        flow = xsend[step, own]
        for k, (away, d) in enumerate(peers):
            slot = (1 + away) * NZ + turned(d)
            x_copy(own, slot, (seg, turned(d)), k).wait_recv()
            flow = flow + xrecv[step, slot]
        old = den[...]
        den[...] = old - relax_factor * (flow + 0.5 * old + layered)

        wait_sent(msg_copy)
        for k in range(11):
            x_copy(own, own, (partner, z), k).wait_send()

    for step, msg in enumerate((msg_first, msg_second)):
        one_step(step, msg)
    wait_sent(wall_copy)

    for c in range(OWN):
        for k in range(3):
            r = 3 * c + k
            pos_out[c, pl.ds(k, 1), :] = pos[pl.ds(r, 1), :]
            vel_out[c, pl.ds(k, 1), :] = vel[pl.ds(r, 1), :]
            den_out[c, pl.ds(k, 1), :] = den[pl.ds(r, 1), :]


def body(
    positions,
    rest_shape,
    modulus,
    stiffness,
    wall_points,
    density,
    wall_operator,
    seg_count,
    neighbours,
    near_patches,
):
    nseg = lax.axis_size("seg")
    vmem = pl.BlockSpec(memory_space=pltpu.VMEM)
    smem = pl.BlockSpec(memory_space=pltpu.SMEM)
    shape = jax.ShapeDtypeStruct((OWN, 3, N), f32)
    dma = pltpu.SemaphoreType.DMA
    return pl.pallas_call(
        functools.partial(fused, nseg),
        out_shape=(shape, shape, shape),
        in_specs=[vmem, vmem, smem, vmem, vmem, vmem, vmem, smem, smem, smem],
        out_specs=(vmem, vmem, vmem),
        scratch_shapes=[
            pltpu.VMEM((SLOTS, ROWS, N), f32),
            pltpu.VMEM((SLOTS, ROWS, N), f32),
            pltpu.VMEM((SLOTS, 16, N), f32),
            pltpu.VMEM((STEPS, SLOTS, 16, N), f32),
            pltpu.VMEM((STEPS, SLOTS, 16, N), f32),
            pltpu.VMEM((PAIRS, N, N), bf16),
            pltpu.VMEM((2, N, N), bf16),
            pltpu.VMEM((OWN, 48, N), bf16),
            pltpu.VMEM((OWN, 48, N), bf16),
            pltpu.VMEM((OWN, 16, N), f32),
            pltpu.VMEM((16, N), f32),
            pltpu.VMEM((16, N), f32),
            pltpu.VMEM((16, N), f32),
            pltpu.VMEM((16, N), f32),
            pltpu.VMEM((16, N), f32),
            pltpu.VMEM((3 * PAIRS, N), f32),
            pltpu.VMEM((SLOTS * 16, 128), bf16),
            pltpu.VMEM((N, N), bf16),
            pltpu.VMEM((N, N), bf16),
            dma((STEPS, 11)),
            dma((STEPS, SLOTS)),
            dma((11,)),
            dma((SLOTS,)),
            dma((STEPS, 11)),
            dma((STEPS, SLOTS)),
        ],
        compiler_params=pltpu.CompilerParams(collective_id=0, has_side_effects=True),
        name="red_cell_steps",
    )(
        positions,
        rest_shape,
        modulus,
        stiffness,
        wall_points,
        density,
        wall_operator,
        seg_count,
        neighbours,
        near_patches,
    )


def solution(mesh):
    placed = (
        P(("seg", "cell"), None, None),
        P(("seg", "cell"), None, None),
        P(("seg", "cell")),
        P(),
        P(("seg", "cell"), None, None),
        P(("seg", "cell"), None, None),
        P(),
        P("seg"),
        P(("seg", "cell"), None),
        P(("seg", "cell"), None),
    )
    return jax.shard_map(
        body,
        mesh=mesh,
        in_specs=placed,
        out_specs=(
            P(("seg", "cell"), None, None),
            P(("seg", "cell"), None, None),
            P(("seg", "cell"), None, None),
        ),
        check_vma=False,
    )
```

```python
import functools

import jax
import jax.numpy as jnp
from jax import lax
from jax.experimental import pallas as pl
from jax.experimental.pallas import tpu as pltpu
from jax.sharding import PartitionSpec as P

N = 512
OWN = 4
NZ = 4
NB = 4
NW = 2
STEPS = 2
SLOTS = 3 * NZ
PAIRS = OWN * NW

soften_square = 0.25
stokes_factor = 0.039788735772973836
relax_factor = 0.5
time_step = 0.5

f32, bf16 = jnp.float32, jnp.bfloat16
MESH = pl.DeviceIdType.MESH


def split3(v):
    a = v.astype(bf16).astype(f32)
    r = v - a
    b = r.astype(bf16).astype(f32)
    return a, b, r - b


def rows8(rows):
    index = lax.broadcasted_iota(jnp.int32, (8, N), 0)
    out = jnp.zeros((8, N), f32)
    for k, row in enumerate(rows):
        out = jnp.where(index == k, jnp.broadcast_to(row, (8, N)), out)
    return out


def dot3(a, b):
    return a[0] * b[0] + a[1] * b[1] + a[2] * b[2]


def source_factor(y):
    p = dot3(y, y)
    a, b, c = split3(rows8([-2.0 * y[0], -2.0 * y[1], -2.0 * y[2], jnp.ones_like(p), p]))
    return jnp.concatenate([a, a, b, a, b, c], 0).astype(bf16)


def target_factor(x):
    q = dot3(x, x) + soften_square
    a, b, c = split3(rows8([x[0], x[1], x[2], q, jnp.ones_like(q)]))
    return jnp.concatenate([a, b, a, c, b, a], 0).astype(bf16)


def moments(y, f):
    p, g = dot3(y, y), dot3(y, f)
    one = rows8([f[0], f[1], f[2], g] + [p * f[k] + g * y[k] for k in range(3)] + [f[0] * y[0]])
    two = rows8([f[l] * y[k] for l in range(3) for k in range(3)][1:])
    a, b, c = split3(jnp.concatenate([one, two], 0))
    return jnp.concatenate([a, b, c], 0).astype(bf16)


def fold(sums):
    return sums[0:16] + sums[16:32] + sums[32:48]


def combine(sums, x):
    row = [sums[k : k + 1] for k in range(16)]
    q = dot3(x, x) + soften_square
    m, g, h = row[0:3], row[3], row[4:7]
    t = [row[7 + 3 * l : 10 + 3 * l] for l in range(3)]
    along = dot3(x, m) - g
    return [
        stokes_factor
        * (
            q * m[k]
            - 2.0 * dot3(x, t[k])
            + h[k]
            + x[k] * along
            - (x[0] * t[0][k] + x[1] * t[1][k] + x[2] * t[2][k])
        )
        for k in range(3)
    ]


def kernel_tile(squares):
    inverse = lax.rsqrt(jnp.maximum(squares, soften_square))
    return (inverse * inverse * inverse).astype(bf16)


def mm(a, b):
    return jnp.dot(a, b, preferred_element_type=f32)


def mt(a, b):
    return lax.dot_general(a, b, (((1,), (1,)), ((), ())), preferred_element_type=f32)


def fused(
    nseg,
    pos_in,
    rest_in,
    modulus,
    stiffness,
    points_in,
    density_in,
    operator,
    seg_count,
    neighbours,
    near,
    pos_out,
    vel_out,
    den_out,
    wall,
    cells_first,
    cells_second,
    den_first,
    den_second,
    xsend,
    xrecv,
    pmat,
    pbuf,
    gcell,
    bcell,
    acc,
    pos,
    rest,
    force,
    den,
    vel,
    pieces,
    onehot,
    op1,
    op2,
    send_sem,
    recv_sem,
    x_send,
    x_recv,
):
    seg = lax.axis_index("seg")
    z = lax.axis_index("cell")
    odd = seg % 2
    partner = seg + 1 - 2 * odd
    across = (seg + 2 * odd - 1 + nseg) % nseg
    own = NZ + z

    def turned(d):
        return (z + d) % NZ

    peers = []
    for away in (0, 1, -1):
        for d in range(NZ):
            if away or d:
                peers.append((away, d))

    barrier = pltpu.get_barrier_semaphore()
    for away, d in peers:
        pl.semaphore_signal(
            barrier, inc=1, device_id=((seg + away + nseg) % nseg, turned(d)), device_id_type=MESH
        )

    for ref in (pos, rest, force, den, vel):
        ref[...] = jnp.zeros_like(ref)
    for k in range(3):
        at = pl.ds(4 * k, 4)
        pos[at, :] = pos_in[k]
        rest[at, :] = rest_in[k]
        den[at, :] = density_in[k]
        wall[own, at, :] = points_in[k]

    item16 = lax.bitwise_and(lax.broadcasted_iota(jnp.int32, (16, N), 0), 3)
    alive = jnp.zeros((16, N), f32)
    scale = jnp.zeros((16, N), f32)
    for c in range(OWN):
        one = jnp.where(z * OWN + c < seg_count[0], 1.0, 0.0).astype(f32)
        alive = jnp.where(item16 == c, one, alive)
        scale = jnp.where(item16 == c, one * modulus[c], scale)

    class Message:
        def __init__(self, buffer, number):
            self.buffer, self.number = buffer, number

        def copy(self, source, target, device, k):
            return pltpu.make_async_remote_copy(
                src_ref=self.buffer.at[source],
                dst_ref=self.buffer.at[target],
                send_sem=send_sem.at[self.number, k],
                recv_sem=recv_sem.at[self.number, target],
                device_id=device,
                device_id_type=MESH,
            )

        def start(self):
            for k, d in enumerate((1, 3, 2)):
                self.copy(own, own, (seg, turned(d)), k).start()
            self.copy(own, 8 - 8 * odd + z, (across, z), 4).start()
            self.copy(own, 8 * odd + z, (partner, z), 3).start()

        def relay(self, *which):
            for d in which:
                slot = NZ + turned(d)
                self.copy(slot, slot, (seg, turned(d)), 0).wait_recv()
                self.copy(slot, 8 - 8 * odd + turned(d), (across, z), 3 + 2 * d).start()
                self.copy(slot, 8 * odd + turned(d), (partner, z), 4 + 2 * d).start()

        def arrived(self):
            for d in range(NZ):
                for base in (0, 8):
                    slot = base + turned(d)
                    self.copy(slot, slot, (partner, z), 0).wait_recv()

        def sent(self):
            for k in range(11):
                self.copy(own, own, (partner, z), k).wait_send()

    walls = Message(wall, 0)
    cell_messages = [Message(cells_first, 1), Message(cells_second, 2)]
    den_messages = [Message(den_first, 3), Message(den_second, 4)]
    first = (seg - 1) * OWN * NZ

    def rows_of(ref, item):
        return [ref[pl.ds(4 * k + item, 1), :] for k in range(3)]

    def rows_at(ref, slot, item, base=0):
        return [ref[slot, pl.ds(base + 4 * k + item, 1), :] for k in range(3)]

    def place(number):
        relative = jnp.clip(number - first, 0, SLOTS * OWN - 1)
        return lax.shift_right_logical(relative, 2), lax.bitwise_and(relative, 3)

    def tiles(source, target, ref, index):
        for k in range(4):
            ref[index, pl.ds(k * 128, 128), :] = kernel_tile(
                mm(source[k * 128 : (k + 1) * 128], target)
            )

    def make_forces():
        offset = (pos[...] - rest[...]).astype(bf16)
        force[...] = mt(offset, stiffness[...]) * scale

    def pack(step):
        buffer = cell_messages[step].buffer
        buffer[own, 0:12, :] = pos[0:12, :]
        buffer[own, 12:24, :] = force[0:12, :]
        den_messages[step].buffer[own] = den[0:12, :]

    def itself():
        for c in range(OWN):
            x, f = rows_of(pos, c), rows_of(force, c)
            g, b = moments(x, f), target_factor(x)
            gcell[c] = g
            bcell[c] = b
            tiles(source_factor(x).T, b, pbuf, c)
            acc[c] = fold(mm(g, pbuf[c]))

    def by_halves(work, between):
        def trip(h, _):
            work(2 * h)

            @pl.when(h == 0)
            def _():
                between()

            return 0

        lax.fori_loop(0, 2, trip, 0)

    def reverse(cell):
        for i in range(2):
            for w in range(NW):
                c = cell + i
                slot, item = place(near[w, c])
                y = rows_at(wall, slot, item)
                pair = c * NW + w
                tiles(source_factor(y).T, bcell[c], pmat, pair)
                out = combine(fold(mt(gcell[c], pmat[pair])), y)
                for k in range(3):
                    pieces[pl.ds(3 * pair + k, 1), :] = out[k]

    def listed(step, cell):
        ref = cell_messages[step].buffer
        for i in range(2):
            c = cell + i
            b = bcell[c]
            sums = None
            for n in range(1, NB):
                slot, item = place(neighbours[c, n])
                y, f = rows_at(ref, slot, item), rows_at(ref, slot, item, 12)
                buffer = i * 3 + n - 1
                tiles(source_factor(y).T, b, pbuf, buffer)
                part = mm(moments(y, f), pbuf[buffer])
                sums = part if sums is None else sums + part
            acc[c] = acc[c] + fold(sums)

    def from_walls(step, cell):
        for i in range(2):
            c = cell + i
            sums = None
            for w in range(NW):
                slot, item = place(near[w, c])
                y, f = rows_at(wall, slot, item), rows_at(den_messages[step].buffer, slot, item)
                part = mm(moments(y, f), pmat[c * NW + w])
                sums = part if sums is None else sums + part
            out = combine(acc[c] + fold(sums), rows_of(pos, c))
            for k in range(3):
                vel[pl.ds(4 * k + c, 1), :] = out[k]

    def x_copy(step, group, target, device, k):
        return pltpu.make_async_remote_copy(
            src_ref=xsend.at[step, group],
            dst_ref=xrecv.at[step, target],
            send_sem=x_send.at[step, k],
            recv_sem=x_recv.at[step, target],
            device_id=device,
            device_id_type=MESH,
        )

    def send_pieces(step):
        high, middle, low = split3(pieces[...])
        spread = jnp.concatenate([high, middle, low, jnp.zeros((56, N), f32)], 0).astype(bf16)
        shares = mm(onehot[...], spread)
        for g in range(SLOTS):
            xsend[step, g] = shares[g * 16 : g * 16 + 12]
        for k, (away, d) in enumerate(peers):
            x_copy(
                step,
                (away + 1) * NZ + turned(d),
                (1 - away) * NZ + z,
                ((seg + away + nseg) % nseg, turned(d)),
                k,
            ).start()

    def operate():
        high, middle, low = split3(den[...])
        layered = fold(mt(jnp.concatenate([high, middle, low], 0).astype(bf16), op1[...]))
        second = mt(jnp.concatenate([high, middle], 0).astype(bf16), op2[...])
        return layered + second[0:16] + second[16:32]

    def move():
        speed = alive * vel[...]
        vel[...] = speed
        pos[...] = pos[...] + time_step * speed

    def update_density(step, layered):
        flow = xsend[step, own]
        for k, (away, d) in enumerate(peers):
            slot = (1 + away) * NZ + turned(d)
            x_copy(step, own, slot, (seg, turned(d)), k).wait_recv()
            flow = flow + xrecv[step, slot]
        old = den[0:12, :]
        den[0:12, :] = old - relax_factor * (flow + 0.5 * old + layered[0:12])

    def cut(i, _):
        at = pl.ds(pl.multiple_of(i * 64, 64), 64)
        whole = operator[at, :]
        high = whole.astype(bf16)
        op1[at, :] = high
        op2[at, :] = (whole - high.astype(f32)).astype(bf16)
        return 0

    def choose():
        hot_row = lax.broadcasted_iota(jnp.int32, (16, 128), 0)
        hot_col = lax.broadcasted_iota(jnp.int32, (16, 128), 1)
        row_item, row_part = lax.bitwise_and(hot_row, 3), lax.shift_right_logical(hot_row, 2)
        col = hot_col - jnp.where(hot_col >= 24, 24, 0) - jnp.where(hot_col >= 48, 24, 0)
        col_pair = lax.shift_right_logical(col * 43, 7)
        col_part = col - 3 * col_pair
        wanted = jnp.full((16, 128), -1, jnp.int32)
        for c in range(OWN):
            for w in range(NW):
                wanted = jnp.where(col_pair == c * NW + w, near[w, c] - first, wanted)
        fits = (row_part == col_part) & (hot_col < 72)
        for g in range(SLOTS):
            hit = fits & (row_item + g * OWN == wanted)
            onehot[pl.ds(g * 16, 16), :] = jnp.where(hit, 1.0, 0.0).astype(bf16)

    make_forces()
    pack(0)
    choose()
    lax.fori_loop(0, N // 64, cut, 0)

    pl.semaphore_wait(barrier, len(peers))
    walls.start()
    cell_messages[0].start()
    itself()
    walls.relay(1, 3, 2)
    den_messages[0].start()
    walls.arrived()
    cell_messages[0].relay(1, 3)

    for step in range(STEPS):
        cells, dens = cell_messages[step], den_messages[step]
        if step == 1:
            make_forces()
            pack(step)
            cells.start()
            dens.start()
            itself()
            by_halves(reverse, lambda: cells.relay(1, 3))
        else:
            by_halves(reverse, lambda: cells.relay(2))
        if step == 1:
            cells.relay(2)
        send_pieces(step)
        dens.relay(1, 3)
        layered = operate()
        dens.relay(2)
        cells.arrived()
        by_halves(functools.partial(listed, step), lambda: None)
        dens.arrived()
        by_halves(functools.partial(from_walls, step), lambda: None)
        move()
        update_density(step, layered)

    walls.sent()
    for step in range(STEPS):
        cell_messages[step].sent()
        den_messages[step].sent()
        for k in range(11):
            x_copy(step, own, own, (partner, z), k).wait_send()

    for k in range(3):
        at = pl.ds(4 * k, 4)
        pos_out[k] = pos[at, :]
        vel_out[k] = vel[at, :]
        den_out[k] = den[at, :]


def body(
    positions,
    rest_shape,
    modulus,
    stiffness,
    wall_points,
    density,
    wall_operator,
    seg_count,
    neighbours,
    near_patches,
):
    nseg = lax.axis_size("seg")
    vmem = pl.BlockSpec(memory_space=pltpu.VMEM)
    smem = pl.BlockSpec(memory_space=pltpu.SMEM)
    shape = jax.ShapeDtypeStruct((3, OWN, N), f32)
    dma = pltpu.SemaphoreType.DMA

    def turn(array):
        return jnp.transpose(array, (1, 0, 2))

    outs = pl.pallas_call(
        functools.partial(fused, nseg),
        out_shape=(shape, shape, shape),
        in_specs=[vmem, vmem, smem, vmem, vmem, vmem, vmem, smem, smem, smem],
        out_specs=(vmem, vmem, vmem),
        scratch_shapes=[
            pltpu.VMEM((SLOTS, 12, N), f32),
            pltpu.VMEM((SLOTS, 24, N), f32),
            pltpu.VMEM((SLOTS, 24, N), f32),
            pltpu.VMEM((SLOTS, 12, N), f32),
            pltpu.VMEM((SLOTS, 12, N), f32),
            pltpu.VMEM((STEPS, SLOTS, 12, N), f32),
            pltpu.VMEM((STEPS, SLOTS, 12, N), f32),
            pltpu.VMEM((PAIRS, N, N), bf16),
            pltpu.VMEM((6, N, N), bf16),
            pltpu.VMEM((OWN, 48, N), bf16),
            pltpu.VMEM((OWN, 48, N), bf16),
            pltpu.VMEM((OWN, 16, N), f32),
            pltpu.VMEM((16, N), f32),
            pltpu.VMEM((16, N), f32),
            pltpu.VMEM((16, N), f32),
            pltpu.VMEM((16, N), f32),
            pltpu.VMEM((16, N), f32),
            pltpu.VMEM((3 * PAIRS, N), f32),
            pltpu.VMEM((SLOTS * 16, 128), bf16),
            pltpu.VMEM((N, N), bf16),
            pltpu.VMEM((N, N), bf16),
            dma((5, 11)),
            dma((5, SLOTS)),
            dma((STEPS, 11)),
            dma((STEPS, SLOTS)),
        ],
        compiler_params=pltpu.CompilerParams(collective_id=0, has_side_effects=True),
        name="red_cell_steps",
    )(
        turn(positions),
        turn(rest_shape),
        modulus,
        stiffness,
        turn(wall_points),
        turn(density),
        wall_operator,
        seg_count,
        neighbours,
        near_patches.T,
    )
    return tuple(turn(out) for out in outs)


def solution(mesh):
    placed = (
        P(("seg", "cell"), None, None),
        P(("seg", "cell"), None, None),
        P(("seg", "cell")),
        P(),
        P(("seg", "cell"), None, None),
        P(("seg", "cell"), None, None),
        P(),
        P("seg"),
        P(("seg", "cell"), None),
        P(("seg", "cell"), None),
    )
    return jax.shard_map(
        body,
        mesh=mesh,
        in_specs=placed,
        out_specs=(
            P(("seg", "cell"), None, None),
            P(("seg", "cell"), None, None),
            P(("seg", "cell"), None, None),
        ),
        check_vma=False,
    )
```

```python
import functools

import jax
import jax.numpy as jnp
from jax import lax
from jax.experimental import pallas as pl
from jax.experimental.pallas import tpu as pltpu
from jax.sharding import PartitionSpec as P

N = 512
OWN = 4
NZ = 4
NB = 4
NW = 2
STEPS = 2
SLOTS = 3 * NZ
PAIRS = OWN * NW

soften_square = 0.25
stokes_factor = 0.039788735772973836
relax_factor = 0.5
time_step = 0.5

f32, bf16 = jnp.float32, jnp.bfloat16
MESH = pl.DeviceIdType.MESH


def split3(v):
    a = v.astype(bf16).astype(f32)
    r = v - a
    b = r.astype(bf16).astype(f32)
    return a, b, r - b


def rows8(rows):
    index = lax.broadcasted_iota(jnp.int32, (8, N), 0)
    out = jnp.zeros((8, N), f32)
    for k, row in enumerate(rows):
        out = jnp.where(index == k, jnp.broadcast_to(row, (8, N)), out)
    return out


def dot3(a, b):
    return a[0] * b[0] + a[1] * b[1] + a[2] * b[2]


def source_factor(y):
    p = dot3(y, y)
    a, b, c = split3(rows8([-2.0 * y[0], -2.0 * y[1], -2.0 * y[2], jnp.ones_like(p), p]))
    return jnp.concatenate([a, a, b, a, b, c], 0).astype(bf16)


def target_factor(x):
    q = dot3(x, x) + soften_square
    a, b, c = split3(rows8([x[0], x[1], x[2], q, jnp.ones_like(q)]))
    return jnp.concatenate([a, b, a, c, b, a], 0).astype(bf16)


def moments(y, f):
    p, g = dot3(y, y), dot3(y, f)
    one = rows8([f[0], f[1], f[2], g] + [p * f[k] + g * y[k] for k in range(3)] + [f[0] * y[0]])
    two = rows8([f[l] * y[k] for l in range(3) for k in range(3)][1:])
    a, b, c = split3(jnp.concatenate([one, two], 0))
    return jnp.concatenate([a, b, c], 0).astype(bf16)


def fold(sums):
    return sums[0:16] + sums[16:32] + sums[32:48]


def combine(sums, x):
    row = [sums[k : k + 1] for k in range(16)]
    q = dot3(x, x) + soften_square
    m, g, h = row[0:3], row[3], row[4:7]
    t = [row[7 + 3 * l : 10 + 3 * l] for l in range(3)]
    along = dot3(x, m) - g
    return [
        stokes_factor
        * (
            q * m[k]
            - 2.0 * dot3(x, t[k])
            + h[k]
            + x[k] * along
            - (x[0] * t[0][k] + x[1] * t[1][k] + x[2] * t[2][k])
        )
        for k in range(3)
    ]


def kernel_tile(squares):
    inverse = lax.rsqrt(squares)
    return (inverse * inverse * inverse).astype(bf16)


def mm(a, b):
    return jnp.dot(a, b, preferred_element_type=f32)


def mt(a, b):
    return lax.dot_general(a, b, (((1,), (1,)), ((), ())), preferred_element_type=f32)


def fused(
    nseg,
    pos_in,
    rest_in,
    modulus,
    stiffness,
    points_in,
    density_in,
    operator,
    seg_count,
    neighbours,
    near,
    pos_out,
    vel_out,
    den_out,
    wall,
    cells_first,
    cells_second,
    den_first,
    den_second,
    xsend,
    xrecv,
    pmat,
    pbuf,
    gcell,
    bcell,
    acc,
    pos,
    rest,
    force,
    den,
    vel,
    pieces,
    onehot,
    op1,
    op2,
    send_sem,
    recv_sem,
    x_send,
    x_recv,
):
    seg = lax.axis_index("seg")
    z = lax.axis_index("cell")
    odd = seg % 2
    partner = seg + 1 - 2 * odd
    across = (seg + 2 * odd - 1 + nseg) % nseg
    own = NZ + z

    def turned(d):
        return (z + d) % NZ

    peers = []
    for away in (0, 1, -1):
        for d in range(NZ):
            if away or d:
                peers.append((away, d))

    barrier = pltpu.get_barrier_semaphore()
    for away, d in peers:
        pl.semaphore_signal(
            barrier, inc=1, device_id=((seg + away + nseg) % nseg, turned(d)), device_id_type=MESH
        )

    for ref in (pos, rest, force, den, vel):
        ref[...] = jnp.zeros_like(ref)
    for k in range(3):
        at = pl.ds(4 * k, 4)
        pos[at, :] = pos_in[k]
        rest[at, :] = rest_in[k]
        den[at, :] = density_in[k]
        wall[own, at, :] = points_in[k]

    item16 = lax.bitwise_and(lax.broadcasted_iota(jnp.int32, (16, N), 0), 3)
    alive = jnp.zeros((16, N), f32)
    scale = jnp.zeros((16, N), f32)
    for c in range(OWN):
        one = jnp.where(z * OWN + c < seg_count[0], 1.0, 0.0).astype(f32)
        alive = jnp.where(item16 == c, one, alive)
        scale = jnp.where(item16 == c, one * modulus[c], scale)

    class Message:
        def __init__(self, buffer, number):
            self.buffer, self.number = buffer, number

        def copy(self, source, target, device, k):
            return pltpu.make_async_remote_copy(
                src_ref=self.buffer.at[source],
                dst_ref=self.buffer.at[target],
                send_sem=send_sem.at[self.number, k],
                recv_sem=recv_sem.at[self.number, target],
                device_id=device,
                device_id_type=MESH,
            )

        def start(self):
            for k, d in enumerate((1, 3, 2)):
                self.copy(own, own, (seg, turned(d)), k).start()
            self.copy(own, 8 - 8 * odd + z, (across, z), 4).start()
            self.copy(own, 8 * odd + z, (partner, z), 3).start()

        def relay(self, *which):
            for d in which:
                slot = NZ + turned(d)
                self.copy(slot, slot, (seg, turned(d)), 0).wait_recv()
                self.copy(slot, 8 - 8 * odd + turned(d), (across, z), 3 + 2 * d).start()
                self.copy(slot, 8 * odd + turned(d), (partner, z), 4 + 2 * d).start()

        def arrived(self):
            for d in range(NZ):
                for base in (0, 8):
                    slot = base + turned(d)
                    self.copy(slot, slot, (partner, z), 0).wait_recv()

        def sent(self):
            for k in range(11):
                self.copy(own, own, (partner, z), k).wait_send()

    walls = Message(wall, 0)
    cell_messages = [Message(cells_first, 1), Message(cells_second, 2)]
    den_messages = [Message(den_first, 3), Message(den_second, 4)]
    first = (seg - 1) * OWN * NZ

    def rows_of(ref, item):
        return [ref[pl.ds(4 * k + item, 1), :] for k in range(3)]

    def rows_at(ref, slot, item, base=0):
        return [ref[slot, pl.ds(base + 4 * k + item, 1), :] for k in range(3)]

    def place(number):
        relative = jnp.clip(number - first, 0, SLOTS * OWN - 1)
        return lax.shift_right_logical(relative, 2), lax.bitwise_and(relative, 3)

    def tiles(source, target, ref, index):
        for k in range(4):
            ref[index, pl.ds(k * 128, 128), :] = kernel_tile(
                mm(source[k * 128 : (k + 1) * 128], target)
            )

    def make_forces():
        offset = (pos[...] - rest[...]).astype(bf16)
        force[...] = mt(offset, stiffness[...]) * scale

    def pack(step):
        buffer = cell_messages[step].buffer
        buffer[own, 0:12, :] = pos[0:12, :]
        buffer[own, 12:24, :] = force[0:12, :]
        den_messages[step].buffer[own] = den[0:12, :]

    def itself(cells):
        for c in cells:
            x, f = rows_of(pos, c), rows_of(force, c)
            g, b = moments(x, f), target_factor(x)
            gcell[c] = g
            bcell[c] = b
            tiles(source_factor(x).T, b, pbuf, c)
            acc[c] = fold(mm(g, pbuf[c]))

    def by_halves(work, between):
        def trip(h, _):
            work(2 * h)

            @pl.when(h == 0)
            def _():
                between()

            return 0

        lax.fori_loop(0, 2, trip, 0)

    def reverse(cell):
        for i in range(2):
            for w in range(NW):
                c = cell + i
                slot, item = place(near[w, c])
                y = rows_at(wall, slot, item)
                pair = c * NW + w
                tiles(source_factor(y).T, bcell[c], pmat, pair)
                out = combine(fold(mt(gcell[c], pmat[pair])), y)
                for k in range(3):
                    pieces[pl.ds(3 * pair + k, 1), :] = out[k]

    def listed(step, cell):
        ref = cell_messages[step].buffer
        for i in range(2):
            c = cell + i
            b = bcell[c]
            sums = None
            for n in range(1, NB):
                slot, item = place(neighbours[c, n])
                y, f = rows_at(ref, slot, item), rows_at(ref, slot, item, 12)
                buffer = i * 3 + n - 1
                tiles(source_factor(y).T, b, pbuf, buffer)
                part = mm(moments(y, f), pbuf[buffer])
                sums = part if sums is None else sums + part
            acc[c] = acc[c] + fold(sums)

    def from_walls(step, cell):
        for i in range(2):
            c = cell + i
            sums = None
            for w in range(NW):
                slot, item = place(near[w, c])
                y, f = rows_at(wall, slot, item), rows_at(den_messages[step].buffer, slot, item)
                part = mm(moments(y, f), pmat[c * NW + w])
                sums = part if sums is None else sums + part
            out = combine(acc[c] + fold(sums), rows_of(pos, c))
            for k in range(3):
                vel[pl.ds(4 * k + c, 1), :] = out[k]

    def x_copy(step, group, target, device, k):
        return pltpu.make_async_remote_copy(
            src_ref=xsend.at[step, group],
            dst_ref=xrecv.at[step, target],
            send_sem=x_send.at[step, k],
            recv_sem=x_recv.at[step, target],
            device_id=device,
            device_id_type=MESH,
        )

    def send_pieces(step):
        high, middle, low = split3(pieces[...])
        spread = jnp.concatenate([high, middle, low, jnp.zeros((56, N), f32)], 0).astype(bf16)
        shares = mm(onehot[...], spread)
        for g in range(SLOTS):
            xsend[step, g] = shares[g * 16 : g * 16 + 12]
        for k, (away, d) in enumerate(peers):
            x_copy(
                step,
                (away + 1) * NZ + turned(d),
                (1 - away) * NZ + z,
                ((seg + away + nseg) % nseg, turned(d)),
                k,
            ).start()

    def operate():
        high, middle, low = split3(den[...])
        layered = fold(mt(jnp.concatenate([high, middle, low], 0).astype(bf16), op1[...]))
        second = mt(jnp.concatenate([high, middle], 0).astype(bf16), op2[...])
        return layered + second[0:16] + second[16:32]

    def move():
        speed = alive * vel[...]
        vel[...] = speed
        pos[...] = pos[...] + time_step * speed

    def update_density(step, layered):
        flow = xsend[step, own]
        for k, (away, d) in enumerate(peers):
            slot = (1 + away) * NZ + turned(d)
            x_copy(step, own, slot, (seg, turned(d)), k).wait_recv()
            flow = flow + xrecv[step, slot]
        old = den[0:12, :]
        den[0:12, :] = old - relax_factor * (flow + 0.5 * old + layered[0:12])

    def cut(i, _):
        at = pl.ds(pl.multiple_of(i * 64, 64), 64)
        whole = operator[at, :]
        high = whole.astype(bf16)
        op1[at, :] = high
        op2[at, :] = (whole - high.astype(f32)).astype(bf16)
        return 0

    def choose():
        hot_row = lax.broadcasted_iota(jnp.int32, (16, 128), 0)
        hot_col = lax.broadcasted_iota(jnp.int32, (16, 128), 1)
        row_item, row_part = lax.bitwise_and(hot_row, 3), lax.shift_right_logical(hot_row, 2)
        col = hot_col - jnp.where(hot_col >= 24, 24, 0) - jnp.where(hot_col >= 48, 24, 0)
        col_pair = lax.shift_right_logical(col * 43, 7)
        col_part = col - 3 * col_pair
        wanted = jnp.full((16, 128), -1, jnp.int32)
        for c in range(OWN):
            for w in range(NW):
                wanted = jnp.where(col_pair == c * NW + w, near[w, c] - first, wanted)
        fits = (row_part == col_part) & (hot_col < 72)
        for g in range(SLOTS):
            hit = fits & (row_item + g * OWN == wanted)
            onehot[pl.ds(g * 16, 16), :] = jnp.where(hit, 1.0, 0.0).astype(bf16)

    pl.semaphore_wait(barrier, len(peers))
    walls.start()
    make_forces()
    pack(0)
    cell_messages[0].start()
    itself((0, 1))
    walls.relay(1, 3)
    itself((2, 3))
    walls.relay(2)
    den_messages[0].start()
    choose()
    cell_messages[0].relay(1, 3)
    lax.fori_loop(0, N // 64, cut, 0)
    cell_messages[0].relay(2)
    walls.arrived()

    for step in range(STEPS):
        cells, dens = cell_messages[step], den_messages[step]
        if step == 0:
            by_halves(reverse, lambda: dens.relay(1, 3))
            dens.relay(2)
        else:
            make_forces()
            pack(step)
            cells.start()
            dens.start()
            itself((0, 1, 2, 3))
            cells.relay(1, 3)

            def between():
                cells.relay(2)
                dens.relay(1, 3)

            by_halves(reverse, between)
            dens.relay(2)
        send_pieces(step)
        layered = operate()
        cells.arrived()
        by_halves(functools.partial(listed, step), lambda: None)
        dens.arrived()
        by_halves(functools.partial(from_walls, step), lambda: None)
        move()
        update_density(step, layered)

    walls.sent()
    for step in range(STEPS):
        cell_messages[step].sent()
        den_messages[step].sent()
        for k in range(11):
            x_copy(step, own, own, (partner, z), k).wait_send()

    for k in range(3):
        at = pl.ds(4 * k, 4)
        pos_out[k] = pos[at, :]
        vel_out[k] = vel[at, :]
        den_out[k] = den[at, :]


def body(
    positions,
    rest_shape,
    modulus,
    stiffness,
    wall_points,
    density,
    wall_operator,
    seg_count,
    neighbours,
    near_patches,
):
    nseg = lax.axis_size("seg")
    vmem = pl.BlockSpec(memory_space=pltpu.VMEM)
    smem = pl.BlockSpec(memory_space=pltpu.SMEM)
    shape = jax.ShapeDtypeStruct((3, OWN, N), f32)
    dma = pltpu.SemaphoreType.DMA

    def turn(array):
        return jnp.transpose(array, (1, 0, 2))

    outs = pl.pallas_call(
        functools.partial(fused, nseg),
        out_shape=(shape, shape, shape),
        in_specs=[vmem, vmem, smem, vmem, vmem, vmem, vmem, smem, smem, smem],
        out_specs=(vmem, vmem, vmem),
        scratch_shapes=[
            pltpu.VMEM((SLOTS, 12, N), f32),
            pltpu.VMEM((SLOTS, 24, N), f32),
            pltpu.VMEM((SLOTS, 24, N), f32),
            pltpu.VMEM((SLOTS, 12, N), f32),
            pltpu.VMEM((SLOTS, 12, N), f32),
            pltpu.VMEM((STEPS, SLOTS, 12, N), f32),
            pltpu.VMEM((STEPS, SLOTS, 12, N), f32),
            pltpu.VMEM((PAIRS, N, N), bf16),
            pltpu.VMEM((6, N, N), bf16),
            pltpu.VMEM((OWN, 48, N), bf16),
            pltpu.VMEM((OWN, 48, N), bf16),
            pltpu.VMEM((OWN, 16, N), f32),
            pltpu.VMEM((16, N), f32),
            pltpu.VMEM((16, N), f32),
            pltpu.VMEM((16, N), f32),
            pltpu.VMEM((16, N), f32),
            pltpu.VMEM((16, N), f32),
            pltpu.VMEM((3 * PAIRS, N), f32),
            pltpu.VMEM((SLOTS * 16, 128), bf16),
            pltpu.VMEM((N, N), bf16),
            pltpu.VMEM((N, N), bf16),
            dma((5, 11)),
            dma((5, SLOTS)),
            dma((STEPS, 11)),
            dma((STEPS, SLOTS)),
        ],
        compiler_params=pltpu.CompilerParams(collective_id=0, has_side_effects=True),
        name="red_cell_steps",
    )(
        turn(positions),
        turn(rest_shape),
        modulus,
        stiffness,
        turn(wall_points),
        turn(density),
        wall_operator,
        seg_count,
        neighbours,
        near_patches.T,
    )
    return tuple(turn(out) for out in outs)


def solution(mesh):
    placed = (
        P(("seg", "cell"), None, None),
        P(("seg", "cell"), None, None),
        P(("seg", "cell")),
        P(),
        P(("seg", "cell"), None, None),
        P(("seg", "cell"), None, None),
        P(),
        P("seg"),
        P(("seg", "cell"), None),
        P(("seg", "cell"), None),
    )
    return jax.shard_map(
        body,
        mesh=mesh,
        in_specs=placed,
        out_specs=(
            P(("seg", "cell"), None, None),
            P(("seg", "cell"), None, None),
            P(("seg", "cell"), None, None),
        ),
        check_vma=False,
    )
```

```python
import functools

import jax
import jax.numpy as jnp
from jax import lax
from jax.experimental import pallas as pl
from jax.experimental.pallas import tpu as pltpu
from jax.sharding import PartitionSpec as P

N = 512
OWN = 4
NZ = 4
NB = 4
NW = 2
STEPS = 2
SLOTS = 3 * NZ
PAIRS = OWN * NW

soften_square = 0.25
stokes_factor = 0.039788735772973836
relax_factor = 0.5
time_step = 0.5

f32, bf16 = jnp.float32, jnp.bfloat16
MESH = pl.DeviceIdType.MESH


def split3(v):
    a = v.astype(bf16).astype(f32)
    r = v - a
    b = r.astype(bf16).astype(f32)
    return a, b, r - b


def rows8(rows):
    index = lax.broadcasted_iota(jnp.int32, (8, N), 0)
    out = jnp.zeros((8, N), f32)
    for k, row in enumerate(rows):
        out = jnp.where(index == k, jnp.broadcast_to(row, (8, N)), out)
    return out


def dot3(a, b):
    return a[0] * b[0] + a[1] * b[1] + a[2] * b[2]


def source_factor(y):
    p = dot3(y, y)
    a, b, c = split3(rows8([-2.0 * y[0], -2.0 * y[1], -2.0 * y[2], jnp.ones_like(p), p]))
    return jnp.concatenate([a, a, b, a, b, c], 0).astype(bf16)


def target_factor(x):
    q = dot3(x, x) + soften_square
    a, b, c = split3(rows8([x[0], x[1], x[2], q, jnp.ones_like(q)]))
    return jnp.concatenate([a, b, a, c, b, a], 0).astype(bf16)


def moments(y, f):
    p, g = dot3(y, y), dot3(y, f)
    one = rows8([f[0], f[1], f[2], g] + [p * f[k] + g * y[k] for k in range(3)] + [f[0] * y[0]])
    two = rows8([f[l] * y[k] for l in range(3) for k in range(3)][1:])
    a, b, c = split3(jnp.concatenate([one, two], 0))
    return jnp.concatenate([a, b, c], 0).astype(bf16)


def fold(sums):
    return sums[0:16] + sums[16:32] + sums[32:48]


def combine(sums, x):
    row = [sums[k : k + 1] for k in range(16)]
    q = dot3(x, x) + soften_square
    m, g, h = row[0:3], row[3], row[4:7]
    t = [row[7 + 3 * l : 10 + 3 * l] for l in range(3)]
    along = dot3(x, m) - g
    return [
        stokes_factor
        * (
            q * m[k]
            - 2.0 * dot3(x, t[k])
            + h[k]
            + x[k] * along
            - (x[0] * t[0][k] + x[1] * t[1][k] + x[2] * t[2][k])
        )
        for k in range(3)
    ]


def kernel_tile(squares):
    inverse = lax.rsqrt(squares)
    return (inverse * inverse * inverse).astype(bf16)


def mm(a, b):
    return jnp.dot(a, b, preferred_element_type=f32)


def mt(a, b):
    return lax.dot_general(a, b, (((1,), (1,)), ((), ())), preferred_element_type=f32)


def fused(
    nseg,
    pos_in,
    rest_in,
    modulus,
    stiffness,
    points_in,
    density_in,
    operator,
    seg_count,
    neighbours,
    near,
    pos_out,
    vel_out,
    den_out,
    wall,
    cells_first,
    cells_second,
    den_first,
    den_second,
    xsend,
    xrecv,
    pmat,
    pbuf,
    gcell,
    bcell,
    acc,
    pos,
    rest,
    force,
    den,
    vel,
    pieces,
    onehot,
    op1,
    op2,
    send_sem,
    recv_sem,
    x_send,
    x_recv,
):
    seg = lax.axis_index("seg")
    z = lax.axis_index("cell")
    odd = seg % 2
    partner = seg + 1 - 2 * odd
    own = NZ + z

    def turned(d):
        return (z + d) % NZ

    beside = seg + 2 * odd - 1
    inside = (beside >= 0) & (beside < nseg)
    across = (beside + nseg) % nseg
    toward = 1 - 2 * odd

    same = [(seg, 0, d) for d in (1, 2, 3)]
    near_peers = same + [(partner, toward, d) for d in range(NZ)]
    far_peers = [(across, -toward, d) for d in range(NZ)]

    barrier = pltpu.get_barrier_semaphore()

    def greet(peers):
        for segment, _, d in peers:
            pl.semaphore_signal(
                barrier, inc=1, device_id=(segment, turned(d)), device_id_type=MESH
            )

    @pl.when(inside)
    def _():
        greet(far_peers)

    greet(near_peers)

    for ref in (pos, rest, force, den, vel):
        ref[...] = jnp.zeros_like(ref)
    for k in range(3):
        at = pl.ds(4 * k, 4)
        pos[at, :] = pos_in[k]
        rest[at, :] = rest_in[k]
        den[at, :] = density_in[k]
        wall[own, at, :] = points_in[k]

    item16 = lax.bitwise_and(lax.broadcasted_iota(jnp.int32, (16, N), 0), 3)
    alive = jnp.zeros((16, N), f32)
    scale = jnp.zeros((16, N), f32)
    for c in range(OWN):
        one = jnp.where(z * OWN + c < seg_count[0], 1.0, 0.0).astype(f32)
        alive = jnp.where(item16 == c, one, alive)
        scale = jnp.where(item16 == c, one * modulus[c], scale)

    class Message:
        def __init__(self, buffer, number):
            self.buffer, self.number = buffer, number

        def copy(self, source, target, device, k):
            return pltpu.make_async_remote_copy(
                src_ref=self.buffer.at[source],
                dst_ref=self.buffer.at[target],
                send_sem=send_sem.at[self.number, k],
                recv_sem=recv_sem.at[self.number, target],
                device_id=device,
                device_id_type=MESH,
            )

        def start(self):
            for k, d in enumerate((1, 3, 2)):
                self.copy(own, own, (seg, turned(d)), k).start()

            @pl.when(inside)
            def _():
                self.copy(own, 8 - 8 * odd + z, (across, z), 4).start()

            self.copy(own, 8 * odd + z, (partner, z), 3).start()

        def relay(self, *which):
            for d in which:
                slot = NZ + turned(d)
                self.copy(slot, slot, (seg, turned(d)), 0).wait_recv()
                self.hand_on(slot, d)

        def hand_on(self, slot, d):
            @pl.when(inside)
            def _():
                self.copy(slot, 8 - 8 * odd + turned(d), (across, z), 3 + 2 * d).start()

            self.copy(slot, 8 * odd + turned(d), (partner, z), 4 + 2 * d).start()

        def arrived(self):
            for d in range(NZ):
                slot = 8 - 8 * odd + turned(d)
                self.copy(slot, slot, (partner, z), 0).wait_recv()

            @pl.when(inside)
            def _():
                for d in range(NZ):
                    slot = 8 * odd + turned(d)
                    self.copy(slot, slot, (partner, z), 0).wait_recv()

        def sent(self):
            for k in (0, 1, 2, 3, 6, 8, 10):
                self.copy(own, own, (partner, z), k).wait_send()

            @pl.when(inside)
            def _():
                for k in (4, 5, 7, 9):
                    self.copy(own, own, (partner, z), k).wait_send()

    walls = Message(wall, 0)
    cell_messages = [Message(cells_first, 1), Message(cells_second, 2)]
    den_messages = [Message(den_first, 3), Message(den_second, 4)]
    first = (seg - 1) * OWN * NZ

    def rows_of(ref, item):
        return [ref[pl.ds(4 * k + item, 1), :] for k in range(3)]

    def rows_at(ref, slot, item, base=0):
        return [ref[slot, pl.ds(base + 4 * k + item, 1), :] for k in range(3)]

    def place(number):
        relative = jnp.clip(number - first, 0, SLOTS * OWN - 1)
        return lax.shift_right_logical(relative, 2), lax.bitwise_and(relative, 3)

    def tiles(source, target, ref, index):
        for k in range(4):
            ref[index, pl.ds(k * 128, 128), :] = kernel_tile(
                mm(source[k * 128 : (k + 1) * 128], target)
            )

    def make_forces():
        offset = (pos[...] - rest[...]).astype(bf16)
        force[...] = mt(offset, stiffness[...]) * scale

    def send_cells(step):
        make_forces()
        buffer = cell_messages[step].buffer
        buffer[own, 0:12, :] = pos[0:12, :]
        buffer[own, 12:24, :] = force[0:12, :]
        cell_messages[step].start()

    def send_density(step):
        den_messages[step].buffer[own] = den[0:12, :]
        den_messages[step].start()

    def itself(cells):
        for c in cells:
            x, f = rows_of(pos, c), rows_of(force, c)
            g, b = moments(x, f), target_factor(x)
            gcell[c] = g
            bcell[c] = b
            tiles(source_factor(x).T, b, pbuf, c)
            acc[c] = fold(mm(g, pbuf[c]))

    def by_halves(work, between):
        def trip(h, _):
            work(2 * h)

            @pl.when(h == 0)
            def _():
                between()

            return 0

        lax.fori_loop(0, 2, trip, 0)

    def reverse(cell):
        for i in range(2):
            for w in range(NW):
                c = cell + i
                slot, item = place(near[w, c])
                y = rows_at(wall, slot, item)
                pair = c * NW + w
                tiles(source_factor(y).T, bcell[c], pmat, pair)
                out = combine(fold(mt(gcell[c], pmat[pair])), y)
                for k in range(3):
                    pieces[pl.ds(3 * pair + k, 1), :] = out[k]

    def listed(step, cell):
        ref = cell_messages[step].buffer
        for i in range(2):
            c = cell + i
            b = bcell[c]
            sums = None
            for n in range(1, NB):
                slot, item = place(neighbours[c, n])
                y, f = rows_at(ref, slot, item), rows_at(ref, slot, item, 12)
                buffer = i * 3 + n - 1
                tiles(source_factor(y).T, b, pbuf, buffer)
                part = mm(moments(y, f), pbuf[buffer])
                sums = part if sums is None else sums + part
            acc[c] = acc[c] + fold(sums)

    def from_walls(step, cell):
        for i in range(2):
            c = cell + i
            sums = None
            for w in range(NW):
                slot, item = place(near[w, c])
                y, f = rows_at(wall, slot, item), rows_at(den_messages[step].buffer, slot, item)
                part = mm(moments(y, f), pmat[c * NW + w])
                sums = part if sums is None else sums + part
            out = combine(acc[c] + fold(sums), rows_of(pos, c))
            for k in range(3):
                vel[pl.ds(4 * k + c, 1), :] = out[k]

    def x_copy(step, group, target, device, k):
        return pltpu.make_async_remote_copy(
            src_ref=xsend.at[step, group],
            dst_ref=xrecv.at[step, target],
            send_sem=x_send.at[step, k],
            recv_sem=x_recv.at[step, target],
            device_id=device,
            device_id_type=MESH,
        )

    def send_pieces(step):
        high, middle, low = split3(pieces[...])
        spread = jnp.concatenate([high, middle, low, jnp.zeros((56, N), f32)], 0).astype(bf16)
        shares = mm(onehot[...], spread)
        for g in range(SLOTS):
            xsend[step, g] = shares[g * 16 : g * 16 + 12]
        @pl.when(inside)
        def _():
            start_shares(step, far_peers, 7)

        start_shares(step, near_peers, 0)

    def start_shares(step, peers, base):
        for k, (segment, away, d) in enumerate(peers):
            x_copy(
                step,
                (away + 1) * NZ + turned(d),
                (1 - away) * NZ + z,
                (segment, turned(d)),
                base + k,
            ).start()

    def operate():
        high, middle, low = split3(den[...])
        layered = fold(mt(jnp.concatenate([high, middle, low], 0).astype(bf16), op1[...]))
        second = mt(jnp.concatenate([high, middle], 0).astype(bf16), op2[...])
        return layered + second[0:16] + second[16:32]

    def move():
        speed = alive * vel[...]
        vel[...] = speed
        pos[...] = pos[...] + time_step * speed

    def update_density(step, layered):
        def taken(peers, flow):
            for _, away, d in peers:
                slot = (1 + away) * NZ + turned(d)
                x_copy(step, own, slot, (partner, z), 0).wait_recv()
                part = xrecv[step, slot]
                flow = part if flow is None else flow + part
            return flow

        flow = taken(near_peers, xsend[step, own])
        old = den[0:12, :]
        den[0:12, :] = old - relax_factor * (flow + 0.5 * old + layered[0:12])

        @pl.when(inside)
        def _():
            den[0:12, :] = den[0:12, :] - relax_factor * taken(far_peers, None)

    def cut(i, _):
        at = pl.ds(pl.multiple_of(i * 64, 64), 64)
        whole = operator[at, :]
        high = whole.astype(bf16)
        op1[at, :] = high
        op2[at, :] = (whole - high.astype(f32)).astype(bf16)
        return 0

    def choose():
        hot_row = lax.broadcasted_iota(jnp.int32, (16, 128), 0)
        hot_col = lax.broadcasted_iota(jnp.int32, (16, 128), 1)
        row_item, row_part = lax.bitwise_and(hot_row, 3), lax.shift_right_logical(hot_row, 2)
        col = hot_col - jnp.where(hot_col >= 24, 24, 0) - jnp.where(hot_col >= 48, 24, 0)
        col_pair = lax.shift_right_logical(col * 43, 7)
        col_part = col - 3 * col_pair
        wanted = jnp.full((16, 128), -1, jnp.int32)
        for c in range(OWN):
            for w in range(NW):
                wanted = jnp.where(col_pair == c * NW + w, near[w, c] - first, wanted)
        fits = (row_part == col_part) & (hot_col < 72)
        for g in range(SLOTS):
            hit = fits & (row_item + g * OWN == wanted)
            onehot[pl.ds(g * 16, 16), :] = jnp.where(hit, 1.0, 0.0).astype(bf16)

    pl.semaphore_wait(
        barrier, jnp.where(inside, len(near_peers) + len(far_peers), len(near_peers))
    )
    walls.start()
    send_cells(0)
    itself((0, 1))
    walls.relay(1, 3)
    itself((2, 3))
    walls.relay(2)
    send_density(0)
    choose()
    cell_messages[0].relay(1, 3)
    lax.fori_loop(0, N // 64, cut, 0)
    cell_messages[0].relay(2)
    layered = operate()
    walls.arrived()

    for step in range(STEPS):
        cells, dens = cell_messages[step], den_messages[step]
        if step == 0:
            by_halves(reverse, lambda: dens.relay(1, 3))
            dens.relay(2)
            send_pieces(step)
        else:
            itself((0, 1, 2, 3))
            cells.relay(1, 3)

            def between():
                cells.relay(2)
                dens.relay(1, 3)

            by_halves(reverse, between)
            dens.relay(2)
            send_pieces(step)
            layered = operate()
        cells.arrived()
        by_halves(functools.partial(listed, step), lambda: None)
        dens.arrived()
        by_halves(functools.partial(from_walls, step), lambda: None)
        move()
        if step + 1 < STEPS:
            send_cells(step + 1)
        update_density(step, layered)
        if step + 1 < STEPS:
            send_density(step + 1)

    walls.sent()
    for step in range(STEPS):
        cell_messages[step].sent()
        den_messages[step].sent()
        for k in range(7):
            x_copy(step, own, own, (partner, z), k).wait_send()

        @pl.when(inside)
        def _():
            for k in range(7, 11):
                x_copy(step, own, own, (partner, z), k).wait_send()

    for k in range(3):
        at = pl.ds(4 * k, 4)
        pos_out[k] = pos[at, :]
        vel_out[k] = vel[at, :]
        den_out[k] = den[at, :]


def body(
    positions,
    rest_shape,
    modulus,
    stiffness,
    wall_points,
    density,
    wall_operator,
    seg_count,
    neighbours,
    near_patches,
):
    nseg = lax.axis_size("seg")
    vmem = pl.BlockSpec(memory_space=pltpu.VMEM)
    smem = pl.BlockSpec(memory_space=pltpu.SMEM)
    shape = jax.ShapeDtypeStruct((3, OWN, N), f32)
    dma = pltpu.SemaphoreType.DMA

    def turn(array):
        return jnp.transpose(array, (1, 0, 2))

    outs = pl.pallas_call(
        functools.partial(fused, nseg),
        out_shape=(shape, shape, shape),
        in_specs=[vmem, vmem, smem, vmem, vmem, vmem, vmem, smem, smem, smem],
        out_specs=(vmem, vmem, vmem),
        scratch_shapes=[
            pltpu.VMEM((SLOTS, 12, N), f32),
            pltpu.VMEM((SLOTS, 24, N), f32),
            pltpu.VMEM((SLOTS, 24, N), f32),
            pltpu.VMEM((SLOTS, 12, N), f32),
            pltpu.VMEM((SLOTS, 12, N), f32),
            pltpu.VMEM((STEPS, SLOTS, 12, N), f32),
            pltpu.VMEM((STEPS, SLOTS, 12, N), f32),
            pltpu.VMEM((PAIRS, N, N), bf16),
            pltpu.VMEM((6, N, N), bf16),
            pltpu.VMEM((OWN, 48, N), bf16),
            pltpu.VMEM((OWN, 48, N), bf16),
            pltpu.VMEM((OWN, 16, N), f32),
            pltpu.VMEM((16, N), f32),
            pltpu.VMEM((16, N), f32),
            pltpu.VMEM((16, N), f32),
            pltpu.VMEM((16, N), f32),
            pltpu.VMEM((16, N), f32),
            pltpu.VMEM((3 * PAIRS, N), f32),
            pltpu.VMEM((SLOTS * 16, 128), bf16),
            pltpu.VMEM((N, N), bf16),
            pltpu.VMEM((N, N), bf16),
            dma((5, 11)),
            dma((5, SLOTS)),
            dma((STEPS, 11)),
            dma((STEPS, SLOTS)),
        ],
        compiler_params=pltpu.CompilerParams(collective_id=0, has_side_effects=True),
        name="red_cell_steps",
    )(
        turn(positions),
        turn(rest_shape),
        modulus,
        stiffness,
        turn(wall_points),
        turn(density),
        wall_operator,
        seg_count,
        neighbours,
        near_patches.T,
    )
    return tuple(turn(out) for out in outs)


def solution(mesh):
    placed = (
        P(("seg", "cell"), None, None),
        P(("seg", "cell"), None, None),
        P(("seg", "cell")),
        P(),
        P(("seg", "cell"), None, None),
        P(("seg", "cell"), None, None),
        P(),
        P("seg"),
        P(("seg", "cell"), None),
        P(("seg", "cell"), None),
    )
    return jax.shard_map(
        body,
        mesh=mesh,
        in_specs=placed,
        out_specs=(
            P(("seg", "cell"), None, None),
            P(("seg", "cell"), None, None),
            P(("seg", "cell"), None, None),
        ),
        check_vma=False,
    )
```

```python
import functools

import jax
import jax.numpy as jnp
from jax import lax
from jax.experimental import pallas as pl
from jax.experimental.pallas import tpu as pltpu
from jax.sharding import PartitionSpec as P

N = 512
OWN = 4
NZ = 4
NB = 4
NW = 2
STEPS = 2
SLOTS = 3 * NZ
PAIRS = OWN * NW

soften_square = 0.25
stokes_factor = 0.039788735772973836
relax_factor = 0.5
time_step = 0.5

f32, bf16 = jnp.float32, jnp.bfloat16
MESH = pl.DeviceIdType.MESH


def split3(v):
    a = v.astype(bf16).astype(f32)
    r = v - a
    b = r.astype(bf16).astype(f32)
    return a, b, r - b


def rows8(rows):
    index = lax.broadcasted_iota(jnp.int32, (8, N), 0)
    out = jnp.zeros((8, N), f32)
    for k, row in enumerate(rows):
        out = jnp.where(index == k, jnp.broadcast_to(row, (8, N)), out)
    return out


def dot3(a, b):
    return a[0] * b[0] + a[1] * b[1] + a[2] * b[2]


def source_factor(y):
    p = dot3(y, y)
    a, b, c = split3(rows8([-2.0 * y[0], -2.0 * y[1], -2.0 * y[2], jnp.ones_like(p), p]))
    return jnp.concatenate([a, a, b, a, b, c], 0).astype(bf16)


def target_factor(x):
    q = dot3(x, x) + soften_square
    a, b, c = split3(rows8([x[0], x[1], x[2], q, jnp.ones_like(q)]))
    return jnp.concatenate([a, b, a, c, b, a], 0).astype(bf16)


def moments(y, f):
    p, g = dot3(y, y), dot3(y, f)
    one = rows8([f[0], f[1], f[2], g] + [p * f[k] + g * y[k] for k in range(3)] + [f[0] * y[0]])
    two = rows8([f[l] * y[k] for l in range(3) for k in range(3)][1:])
    a, b, c = split3(jnp.concatenate([one, two], 0))
    return jnp.concatenate([a, b, c], 0).astype(bf16)


def fold(sums):
    return sums[0:16] + sums[16:32] + sums[32:48]


def combine(sums, x):
    row = [sums[k : k + 1] for k in range(16)]
    q = dot3(x, x) + soften_square
    m, g, h = row[0:3], row[3], row[4:7]
    t = [row[7 + 3 * l : 10 + 3 * l] for l in range(3)]
    along = dot3(x, m) - g
    return [
        stokes_factor
        * (
            q * m[k]
            - 2.0 * dot3(x, t[k])
            + h[k]
            + x[k] * along
            - (x[0] * t[0][k] + x[1] * t[1][k] + x[2] * t[2][k])
        )
        for k in range(3)
    ]


def kernel_tile(squares):
    inverse = lax.rsqrt(squares)
    return (inverse * inverse * inverse).astype(bf16)


def mm(a, b):
    return jnp.dot(a, b, preferred_element_type=f32)


def mt(a, b):
    return lax.dot_general(a, b, (((1,), (1,)), ((), ())), preferred_element_type=f32)


def fused(
    nseg,
    pos_in,
    rest_in,
    modulus,
    stiffness_in,
    points_in,
    density_in,
    operator_in,
    seg_count,
    neighbours,
    near,
    out,
    wall,
    cells_first,
    cells_second,
    den_first,
    den_second,
    xsend,
    xrecv,
    pmat,
    pbuf,
    gcell,
    bcell,
    acc,
    pos,
    rest,
    force,
    den,
    vel,
    pieces,
    onehot,
    op1,
    op2,
    send_sem,
    recv_sem,
    x_send,
    x_recv,
    stiffness,
    operator,
    load_sem,
):
    load_stiffness = pltpu.make_async_copy(stiffness_in, stiffness, load_sem.at[0])
    load_operator = pltpu.make_async_copy(operator_in, operator, load_sem.at[1])
    load_stiffness.start()
    load_operator.start()
    seg = lax.axis_index("seg")
    z = lax.axis_index("cell")
    odd = seg % 2
    partner = seg + 1 - 2 * odd
    own = NZ + z

    def turned(d):
        return (z + d) % NZ

    beside = seg + 2 * odd - 1
    inside = (beside >= 0) & (beside < nseg)
    across = (beside + nseg) % nseg
    toward = 1 - 2 * odd

    same = [(seg, 0, d) for d in (1, 2, 3)]
    near_peers = same + [(partner, toward, d) for d in range(NZ)]
    far_peers = [(across, -toward, d) for d in range(NZ)]

    barrier = pltpu.get_barrier_semaphore()

    def greet(peers):
        for segment, _, d in peers:
            pl.semaphore_signal(
                barrier, inc=1, device_id=(segment, turned(d)), device_id_type=MESH
            )

    @pl.when(inside)
    def _():
        greet(far_peers)

    greet(near_peers)

    for ref in (pos, rest, force, den, vel):
        ref[...] = jnp.zeros_like(ref)
    for k in range(3):
        at = pl.ds(4 * k, 4)
        pos[at, :] = pos_in[k]
        rest[at, :] = rest_in[k]
        den[at, :] = density_in[k]
        wall[own, at, :] = points_in[k]

    item16 = lax.bitwise_and(lax.broadcasted_iota(jnp.int32, (16, N), 0), 3)
    alive = jnp.zeros((16, N), f32)
    scale = jnp.zeros((16, N), f32)
    for c in range(OWN):
        one = jnp.where(z * OWN + c < seg_count[0], 1.0, 0.0).astype(f32)
        alive = jnp.where(item16 == c, one, alive)
        scale = jnp.where(item16 == c, one * modulus[c], scale)

    class Message:
        def __init__(self, buffer, number):
            self.buffer, self.number = buffer, number

        def copy(self, source, target, device, k):
            return pltpu.make_async_remote_copy(
                src_ref=self.buffer.at[source],
                dst_ref=self.buffer.at[target],
                send_sem=send_sem.at[self.number, k],
                recv_sem=recv_sem.at[self.number, target],
                device_id=device,
                device_id_type=MESH,
            )

        def start(self):
            for k, d in enumerate((1, 3, 2)):
                self.copy(own, own, (seg, turned(d)), k).start()

            @pl.when(inside)
            def _():
                self.copy(own, 8 - 8 * odd + z, (across, z), 4).start()

            self.copy(own, 8 * odd + z, (partner, z), 3).start()

        def relay(self, *which):
            for d in which:
                slot = NZ + turned(d)
                self.copy(slot, slot, (seg, turned(d)), 0).wait_recv()
                self.hand_on(slot, d)

        def hand_on(self, slot, d):
            @pl.when(inside)
            def _():
                self.copy(slot, 8 - 8 * odd + turned(d), (across, z), 3 + 2 * d).start()

            self.copy(slot, 8 * odd + turned(d), (partner, z), 4 + 2 * d).start()

        def arrived(self):
            for d in range(NZ):
                slot = 8 - 8 * odd + turned(d)
                self.copy(slot, slot, (partner, z), 0).wait_recv()

            @pl.when(inside)
            def _():
                for d in range(NZ):
                    slot = 8 * odd + turned(d)
                    self.copy(slot, slot, (partner, z), 0).wait_recv()

        def sent(self):
            for k in (0, 1, 2, 3, 6, 8, 10):
                self.copy(own, own, (partner, z), k).wait_send()

            @pl.when(inside)
            def _():
                for k in (4, 5, 7, 9):
                    self.copy(own, own, (partner, z), k).wait_send()

    walls = Message(wall, 0)
    cell_messages = [Message(cells_first, 1), Message(cells_second, 2)]
    den_messages = [Message(den_first, 3), Message(den_second, 4)]
    first = (seg - 1) * OWN * NZ

    def rows_of(ref, item):
        return [ref[pl.ds(4 * k + item, 1), :] for k in range(3)]

    def rows_at(ref, slot, item, base=0):
        return [ref[slot, pl.ds(base + 4 * k + item, 1), :] for k in range(3)]

    def place(number):
        relative = jnp.clip(number - first, 0, SLOTS * OWN - 1)
        return lax.shift_right_logical(relative, 2), lax.bitwise_and(relative, 3)

    def tiles(source, target, ref, index):
        for k in range(4):
            ref[index, pl.ds(k * 128, 128), :] = kernel_tile(
                mm(source[k * 128 : (k + 1) * 128], target)
            )

    def make_forces():
        offset = (pos[...] - rest[...]).astype(bf16)
        force[...] = mt(offset, stiffness[...]) * scale

    def send_cells(step):
        make_forces()
        buffer = cell_messages[step].buffer
        buffer[own, 0:12, :] = pos[0:12, :]
        buffer[own, 12:24, :] = force[0:12, :]
        cell_messages[step].start()

    def send_density(step):
        den_messages[step].buffer[own] = den[0:12, :]
        den_messages[step].start()

    def itself(cells):
        for c in cells:
            x, f = rows_of(pos, c), rows_of(force, c)
            g, b = moments(x, f), target_factor(x)
            gcell[c] = g
            bcell[c] = b
            tiles(source_factor(x).T, b, pbuf, c)
            acc[c] = fold(mm(g, pbuf[c]))

    def by_halves(work, between):
        def trip(h, _):
            work(2 * h)

            @pl.when(h == 0)
            def _():
                between()

            return 0

        lax.fori_loop(0, 2, trip, 0)

    def reverse(cell):
        for i in range(2):
            for w in range(NW):
                c = cell + i
                slot, item = place(near[w, c])
                y = rows_at(wall, slot, item)
                pair = c * NW + w
                tiles(source_factor(y).T, bcell[c], pmat, pair)
                out = combine(fold(mt(gcell[c], pmat[pair])), y)
                for k in range(3):
                    pieces[pl.ds(3 * pair + k, 1), :] = out[k]

    def listed(step, cell):
        ref = cell_messages[step].buffer
        for i in range(2):
            c = cell + i
            b = bcell[c]
            sums = None
            for n in range(1, NB):
                slot, item = place(neighbours[c, n])
                y, f = rows_at(ref, slot, item), rows_at(ref, slot, item, 12)
                buffer = i * 3 + n - 1
                tiles(source_factor(y).T, b, pbuf, buffer)
                part = mm(moments(y, f), pbuf[buffer])
                sums = part if sums is None else sums + part
            acc[c] = acc[c] + fold(sums)

    def from_walls(step, cell):
        for i in range(2):
            c = cell + i
            sums = None
            for w in range(NW):
                slot, item = place(near[w, c])
                y, f = rows_at(wall, slot, item), rows_at(den_messages[step].buffer, slot, item)
                part = mm(moments(y, f), pmat[c * NW + w])
                sums = part if sums is None else sums + part
            out = combine(acc[c] + fold(sums), rows_of(pos, c))
            for k in range(3):
                vel[pl.ds(4 * k + c, 1), :] = out[k]

    def x_copy(step, group, target, device, k):
        return pltpu.make_async_remote_copy(
            src_ref=xsend.at[step, group],
            dst_ref=xrecv.at[step, target],
            send_sem=x_send.at[step, k],
            recv_sem=x_recv.at[step, target],
            device_id=device,
            device_id_type=MESH,
        )

    def send_pieces(step):
        high, middle, low = split3(pieces[...])
        spread = jnp.concatenate([high, middle, low, jnp.zeros((56, N), f32)], 0).astype(bf16)
        shares = mm(onehot[...], spread)
        for g in range(SLOTS):
            xsend[step, g] = shares[g * 16 : g * 16 + 12]
        @pl.when(inside)
        def _():
            start_shares(step, far_peers, 7)

        start_shares(step, near_peers, 0)

    def start_shares(step, peers, base):
        for k, (segment, away, d) in enumerate(peers):
            x_copy(
                step,
                (away + 1) * NZ + turned(d),
                (1 - away) * NZ + z,
                (segment, turned(d)),
                base + k,
            ).start()

    def operate():
        high, middle, low = split3(den[...])
        layered = fold(mt(jnp.concatenate([high, middle, low], 0).astype(bf16), op1[...]))
        second = mt(jnp.concatenate([high, middle], 0).astype(bf16), op2[...])
        return layered + second[0:16] + second[16:32]

    def move():
        speed = alive * vel[...]
        vel[...] = speed
        pos[...] = pos[...] + time_step * speed

    def update_density(step, layered):
        def taken(peers, flow):
            for _, away, d in peers:
                slot = (1 + away) * NZ + turned(d)
                x_copy(step, own, slot, (partner, z), 0).wait_recv()
                part = xrecv[step, slot]
                flow = part if flow is None else flow + part
            return flow

        flow = taken(near_peers, xsend[step, own])
        old = den[0:12, :]
        den[0:12, :] = old - relax_factor * (flow + 0.5 * old + layered[0:12])

        @pl.when(inside)
        def _():
            den[0:12, :] = den[0:12, :] - relax_factor * taken(far_peers, None)

    def cut(i, _):
        at = pl.ds(pl.multiple_of(i * 64, 64), 64)
        whole = operator[at, :]
        high = whole.astype(bf16)
        op1[at, :] = high
        op2[at, :] = (whole - high.astype(f32)).astype(bf16)
        return 0

    def choose():
        hot_row = lax.broadcasted_iota(jnp.int32, (16, 128), 0)
        hot_col = lax.broadcasted_iota(jnp.int32, (16, 128), 1)
        row_item, row_part = lax.bitwise_and(hot_row, 3), lax.shift_right_logical(hot_row, 2)
        col = hot_col - jnp.where(hot_col >= 24, 24, 0) - jnp.where(hot_col >= 48, 24, 0)
        col_pair = lax.shift_right_logical(col * 43, 7)
        col_part = col - 3 * col_pair
        wanted = jnp.full((16, 128), -1, jnp.int32)
        for c in range(OWN):
            for w in range(NW):
                wanted = jnp.where(col_pair == c * NW + w, near[w, c] - first, wanted)
        fits = (row_part == col_part) & (hot_col < 72)
        for g in range(SLOTS):
            hit = fits & (row_item + g * OWN == wanted)
            onehot[pl.ds(g * 16, 16), :] = jnp.where(hit, 1.0, 0.0).astype(bf16)

    pl.semaphore_wait(
        barrier, jnp.where(inside, len(near_peers) + len(far_peers), len(near_peers))
    )
    walls.start()
    load_stiffness.wait()
    send_cells(0)
    itself((0, 1))
    walls.relay(1, 3)
    itself((2, 3))
    walls.relay(2)
    send_density(0)
    choose()
    cell_messages[0].relay(1, 3)
    load_operator.wait()
    lax.fori_loop(0, N // 64, cut, 0)
    cell_messages[0].relay(2)
    layered = operate()
    walls.arrived()

    for step in range(STEPS):
        cells, dens = cell_messages[step], den_messages[step]
        if step == 0:
            by_halves(reverse, lambda: dens.relay(1, 3))
            dens.relay(2)
            send_pieces(step)
        else:
            itself((0, 1, 2, 3))
            cells.relay(1, 3)
            layered = operate()
            cells.relay(2)
            by_halves(reverse, lambda: dens.relay(1, 3))
            dens.relay(2)
            send_pieces(step)
        cells.arrived()
        by_halves(functools.partial(listed, step), lambda: None)
        dens.arrived()
        by_halves(functools.partial(from_walls, step), lambda: None)
        move()
        if step + 1 < STEPS:
            send_cells(step + 1)
        update_density(step, layered)
        if step + 1 < STEPS:
            send_density(step + 1)

    walls.sent()
    for step in range(STEPS):
        cell_messages[step].sent()
        den_messages[step].sent()
        for k in range(7):
            x_copy(step, own, own, (partner, z), k).wait_send()

        @pl.when(inside)
        def _():
            for k in range(7, 11):
                x_copy(step, own, own, (partner, z), k).wait_send()

    for k in range(3):
        at = pl.ds(4 * k, 4)
        out[0, k] = pos[at, :]
        out[1, k] = vel[at, :]
        out[2, k] = den[at, :]


def part_results(state, pos_out, vel_out, den_out):
    for k, ref in enumerate((pos_out, vel_out, den_out)):
        ref[...] = state[k]


def body(
    positions,
    rest_shape,
    modulus,
    stiffness,
    wall_points,
    density,
    wall_operator,
    seg_count,
    neighbours,
    near_patches,
):
    nseg = lax.axis_size("seg")
    vmem = pl.BlockSpec(memory_space=pltpu.VMEM)
    smem = pl.BlockSpec(memory_space=pltpu.SMEM)
    hbm = pl.BlockSpec(memory_space=pl.ANY)
    shape = jax.ShapeDtypeStruct((3, OWN, N), f32)
    dma = pltpu.SemaphoreType.DMA

    def turn(array):
        return jnp.transpose(array, (1, 0, 2))

    state = pl.pallas_call(
        functools.partial(fused, nseg),
        out_shape=jax.ShapeDtypeStruct((3, 3, OWN, N), f32),
        in_specs=[vmem, vmem, smem, hbm, vmem, vmem, hbm, smem, smem, smem],
        out_specs=vmem,
        scratch_shapes=[
            pltpu.VMEM((SLOTS, 12, N), f32),
            pltpu.VMEM((SLOTS, 24, N), f32),
            pltpu.VMEM((SLOTS, 24, N), f32),
            pltpu.VMEM((SLOTS, 12, N), f32),
            pltpu.VMEM((SLOTS, 12, N), f32),
            pltpu.VMEM((STEPS, SLOTS, 12, N), f32),
            pltpu.VMEM((STEPS, SLOTS, 12, N), f32),
            pltpu.VMEM((PAIRS, N, N), bf16),
            pltpu.VMEM((6, N, N), bf16),
            pltpu.VMEM((OWN, 48, N), bf16),
            pltpu.VMEM((OWN, 48, N), bf16),
            pltpu.VMEM((OWN, 16, N), f32),
            pltpu.VMEM((16, N), f32),
            pltpu.VMEM((16, N), f32),
            pltpu.VMEM((16, N), f32),
            pltpu.VMEM((16, N), f32),
            pltpu.VMEM((16, N), f32),
            pltpu.VMEM((3 * PAIRS, N), f32),
            pltpu.VMEM((SLOTS * 16, 128), bf16),
            pltpu.VMEM((N, N), bf16),
            pltpu.VMEM((N, N), bf16),
            dma((5, 11)),
            dma((5, SLOTS)),
            dma((STEPS, 11)),
            dma((STEPS, SLOTS)),
            pltpu.VMEM((N, N), bf16),
            pltpu.VMEM((N, N), f32),
            dma((2,)),
        ],
        compiler_params=pltpu.CompilerParams(collective_id=0, has_side_effects=True),
        name="red_cell_steps",
    )(
        turn(positions),
        turn(rest_shape),
        modulus,
        stiffness,
        turn(wall_points),
        turn(density),
        wall_operator,
        seg_count,
        neighbours,
        near_patches.T,
    )
    outs = pl.pallas_call(
        part_results,
        out_shape=(shape, shape, shape),
        in_specs=[vmem],
        out_specs=(vmem, vmem, vmem),
        name="part_results",
    )(state)
    return tuple(turn(out) for out in outs)


def solution(mesh):
    placed = (
        P(("seg", "cell"), None, None),
        P(("seg", "cell"), None, None),
        P(("seg", "cell")),
        P(),
        P(("seg", "cell"), None, None),
        P(("seg", "cell"), None, None),
        P(),
        P("seg"),
        P(("seg", "cell"), None),
        P(("seg", "cell"), None),
    )
    return jax.shard_map(
        body,
        mesh=mesh,
        in_specs=placed,
        out_specs=(
            P(("seg", "cell"), None, None),
            P(("seg", "cell"), None, None),
            P(("seg", "cell"), None, None),
        ),
        check_vma=False,
    )
```

```python
import functools

import jax
import jax.numpy as jnp
from jax import lax
from jax.experimental import pallas as pl
from jax.experimental.pallas import tpu as pltpu
from jax.sharding import PartitionSpec as P

N = 512
OWN = 4
NZ = 4
NB = 4
NW = 2
STEPS = 2
SLOTS = 3 * NZ
PAIRS = OWN * NW

soften_square = 0.25
stokes_factor = 0.039788735772973836
relax_factor = 0.5
time_step = 0.5

f32, bf16 = jnp.float32, jnp.bfloat16
MESH = pl.DeviceIdType.MESH


def split3(v):
    a = v.astype(bf16).astype(f32)
    r = v - a
    b = r.astype(bf16).astype(f32)
    return a, b, r - b


def rows8(rows):
    rows = list(rows) + [jnp.zeros_like(rows[0])] * (8 - len(rows))
    return jnp.concatenate(rows, 0)


def dot3(a, b):
    return a[0] * b[0] + a[1] * b[1] + a[2] * b[2]


def source_factor(y):
    p = dot3(y, y)
    a, b, c = split3(rows8([-2.0 * y[0], -2.0 * y[1], -2.0 * y[2], jnp.ones_like(p), p]))
    return jnp.concatenate([a, a, b, a, b, c], 0).astype(bf16)


def target_factor(x):
    q = dot3(x, x) + soften_square
    a, b, c = split3(rows8([x[0], x[1], x[2], q, jnp.ones_like(q)]))
    return jnp.concatenate([a, b, a, c, b, a], 0).astype(bf16)


def moments(y, f):
    p, g = dot3(y, y), dot3(y, f)
    one = rows8([f[0], f[1], f[2], g] + [p * f[k] + g * y[k] for k in range(3)] + [f[0] * y[0]])
    two = rows8([f[l] * y[k] for l in range(3) for k in range(3)][1:])
    a, b, c = split3(jnp.concatenate([one, two], 0))
    return jnp.concatenate([a, b, c], 0).astype(bf16)


def fold(sums):
    return sums[0:16] + sums[16:32] + sums[32:48]


def combine(sums, x):
    row = [sums[k : k + 1] for k in range(16)]
    q = dot3(x, x) + soften_square
    m, g, h = row[0:3], row[3], row[4:7]
    t = [row[7 + 3 * l : 10 + 3 * l] for l in range(3)]
    along = dot3(x, m) - g
    return [
        stokes_factor
        * (
            q * m[k]
            - 2.0 * dot3(x, t[k])
            + h[k]
            + x[k] * along
            - (x[0] * t[0][k] + x[1] * t[1][k] + x[2] * t[2][k])
        )
        for k in range(3)
    ]


def kernel_tile(squares):
    inverse = lax.rsqrt(squares)
    return (inverse * inverse * inverse).astype(bf16)


def mm(a, b):
    return jnp.dot(a, b, preferred_element_type=f32)


def mt(a, b):
    return lax.dot_general(a, b, (((1,), (1,)), ((), ())), preferred_element_type=f32)


def fused(
    nseg,
    pos_in,
    rest_in,
    modulus,
    stiffness_in,
    points_in,
    density_in,
    operator_in,
    seg_count,
    neighbours,
    near,
    out,
    wall,
    cells_first,
    cells_second,
    den_first,
    den_second,
    xsend,
    xrecv,
    pmat,
    pbuf,
    gcell,
    bcell,
    acc,
    pos,
    rest,
    force,
    den,
    vel,
    pieces,
    onehot,
    op1,
    op2,
    send_sem,
    recv_sem,
    x_send,
    x_recv,
    stiffness,
    operator,
    load_sem,
):
    load_stiffness = pltpu.make_async_copy(stiffness_in, stiffness, load_sem.at[0])
    load_operator = pltpu.make_async_copy(operator_in, operator, load_sem.at[1])
    load_stiffness.start()
    load_operator.start()
    seg = lax.axis_index("seg")
    z = lax.axis_index("cell")
    odd = seg % 2
    partner = seg + 1 - 2 * odd
    own = NZ + z

    def turned(d):
        return (z + d) % NZ

    beside = seg + 2 * odd - 1
    inside = (beside >= 0) & (beside < nseg)
    across = (beside + nseg) % nseg
    toward = 1 - 2 * odd

    same = [(seg, 0, d) for d in (1, 2, 3)]
    near_peers = same + [(partner, toward, d) for d in range(NZ)]
    far_peers = [(across, -toward, d) for d in range(NZ)]

    barrier = pltpu.get_barrier_semaphore()

    def greet(peers):
        for segment, _, d in peers:
            pl.semaphore_signal(
                barrier, inc=1, device_id=(segment, turned(d)), device_id_type=MESH
            )

    @pl.when(inside)
    def _():
        greet(far_peers)

    greet(near_peers)

    for ref in (pos, rest, force, den, vel):
        ref[...] = jnp.zeros_like(ref)
    for k in range(3):
        at = pl.ds(4 * k, 4)
        pos[at, :] = pos_in[k]
        rest[at, :] = rest_in[k]
        den[at, :] = density_in[k]
        wall[own, at, :] = points_in[k]

    item16 = lax.bitwise_and(lax.broadcasted_iota(jnp.int32, (16, N), 0), 3)
    alive = jnp.zeros((16, N), f32)
    scale = jnp.zeros((16, N), f32)
    for c in range(OWN):
        one = jnp.where(z * OWN + c < seg_count[0], 1.0, 0.0).astype(f32)
        alive = jnp.where(item16 == c, one, alive)
        scale = jnp.where(item16 == c, one * modulus[c], scale)

    class Message:
        def __init__(self, buffer, number):
            self.buffer, self.number = buffer, number

        def copy(self, source, target, device, k):
            return pltpu.make_async_remote_copy(
                src_ref=self.buffer.at[source],
                dst_ref=self.buffer.at[target],
                send_sem=send_sem.at[self.number, k],
                recv_sem=recv_sem.at[self.number, target],
                device_id=device,
                device_id_type=MESH,
            )

        def start(self):
            for k, d in enumerate((1, 3, 2)):
                self.copy(own, own, (seg, turned(d)), k).start()

            @pl.when(inside)
            def _():
                self.copy(own, 8 - 8 * odd + z, (across, z), 4).start()

            self.copy(own, 8 * odd + z, (partner, z), 3).start()

        def relay(self, *which):
            for d in which:
                slot = NZ + turned(d)
                self.copy(slot, slot, (seg, turned(d)), 0).wait_recv()
                self.hand_on(slot, d)

        def hand_on(self, slot, d):
            @pl.when(inside)
            def _():
                self.copy(slot, 8 - 8 * odd + turned(d), (across, z), 3 + 2 * d).start()

            self.copy(slot, 8 * odd + turned(d), (partner, z), 4 + 2 * d).start()

        def arrived(self):
            for d in range(NZ):
                slot = 8 - 8 * odd + turned(d)
                self.copy(slot, slot, (partner, z), 0).wait_recv()

            @pl.when(inside)
            def _():
                for d in range(NZ):
                    slot = 8 * odd + turned(d)
                    self.copy(slot, slot, (partner, z), 0).wait_recv()

        def sent(self):
            for k in (0, 1, 2, 3, 6, 8, 10):
                self.copy(own, own, (partner, z), k).wait_send()

            @pl.when(inside)
            def _():
                for k in (4, 5, 7, 9):
                    self.copy(own, own, (partner, z), k).wait_send()

    walls = Message(wall, 0)
    cell_messages = [Message(cells_first, 1), Message(cells_second, 2)]
    den_messages = [Message(den_first, 3), Message(den_second, 4)]
    first = (seg - 1) * OWN * NZ

    def rows_of(ref, item):
        return [ref[pl.ds(4 * k + item, 1), :] for k in range(3)]

    def rows_at(ref, slot, item, base=0):
        return [ref[slot, pl.ds(base + 4 * k + item, 1), :] for k in range(3)]

    def place(number):
        relative = jnp.clip(number - first, 0, SLOTS * OWN - 1)
        return lax.shift_right_logical(relative, 2), lax.bitwise_and(relative, 3)

    def tiles(source, target, ref, index):
        for k in range(4):
            ref[index, pl.ds(k * 128, 128), :] = kernel_tile(
                mm(source[k * 128 : (k + 1) * 128], target)
            )

    def make_forces():
        offset = (pos[...] - rest[...]).astype(bf16)
        force[...] = mt(offset, stiffness[...]) * scale

    def send_cells(step):
        make_forces()
        buffer = cell_messages[step].buffer
        buffer[own, 0:12, :] = pos[0:12, :]
        buffer[own, 12:24, :] = force[0:12, :]
        cell_messages[step].start()

    def send_density(step):
        den_messages[step].buffer[own] = den[0:12, :]
        den_messages[step].start()

    def itself(cells):
        for c in cells:
            x, f = rows_of(pos, c), rows_of(force, c)
            g, b = moments(x, f), target_factor(x)
            gcell[c] = g
            bcell[c] = b
            tiles(source_factor(x).T, b, pbuf, c)
            acc[c] = fold(mm(g, pbuf[c]))

    def by_halves(work, between):
        work(0)
        between()
        work(2)

    def reverse(cell):
        for i in range(2):
            for w in range(NW):
                c = cell + i
                slot, item = place(near[w, c])
                y = rows_at(wall, slot, item)
                pair = c * NW + w
                tiles(source_factor(y).T, bcell[c], pmat, pair)
                out = combine(fold(mt(gcell[c], pmat[pair])), y)
                for k in range(3):
                    pieces[pl.ds(3 * pair + k, 1), :] = out[k]

    def listed(step, cell):
        ref = cell_messages[step].buffer
        for i in range(2):
            c = cell + i
            b = bcell[c]
            sums = None
            for n in range(1, NB):
                slot, item = place(neighbours[c, n])
                y, f = rows_at(ref, slot, item), rows_at(ref, slot, item, 12)
                buffer = i * 3 + n - 1
                tiles(source_factor(y).T, b, pbuf, buffer)
                part = mm(moments(y, f), pbuf[buffer])
                sums = part if sums is None else sums + part
            acc[c] = acc[c] + fold(sums)

    def from_walls(step, cell):
        for i in range(2):
            c = cell + i
            sums = None
            for w in range(NW):
                slot, item = place(near[w, c])
                y, f = rows_at(wall, slot, item), rows_at(den_messages[step].buffer, slot, item)
                part = mm(moments(y, f), pmat[c * NW + w])
                sums = part if sums is None else sums + part
            out = combine(acc[c] + fold(sums), rows_of(pos, c))
            for k in range(3):
                vel[pl.ds(4 * k + c, 1), :] = out[k]

    def x_copy(step, group, target, device, k):
        return pltpu.make_async_remote_copy(
            src_ref=xsend.at[step, group],
            dst_ref=xrecv.at[step, target],
            send_sem=x_send.at[step, k],
            recv_sem=x_recv.at[step, target],
            device_id=device,
            device_id_type=MESH,
        )

    def send_pieces(step):
        high, middle, low = split3(pieces[...])
        spread = jnp.concatenate([high, middle, low, jnp.zeros((56, N), f32)], 0).astype(bf16)
        shares = mm(onehot[...], spread)
        for g in range(SLOTS):
            xsend[step, g] = shares[g * 16 : g * 16 + 12]
        @pl.when(inside)
        def _():
            start_shares(step, far_peers, 7)

        start_shares(step, near_peers, 0)

    def start_shares(step, peers, base):
        for k, (segment, away, d) in enumerate(peers):
            x_copy(
                step,
                (away + 1) * NZ + turned(d),
                (1 - away) * NZ + z,
                (segment, turned(d)),
                base + k,
            ).start()

    def operate():
        high, middle, low = split3(den[...])
        layered = fold(mt(jnp.concatenate([high, middle, low], 0).astype(bf16), op1[...]))
        second = mt(jnp.concatenate([high, middle], 0).astype(bf16), op2[...])
        return layered + second[0:16] + second[16:32]

    def move():
        speed = alive * vel[...]
        vel[...] = speed
        pos[...] = pos[...] + time_step * speed

    def update_density(step, layered):
        def taken(peers, flow):
            for _, away, d in peers:
                slot = (1 + away) * NZ + turned(d)
                x_copy(step, own, slot, (partner, z), 0).wait_recv()
                part = xrecv[step, slot]
                flow = part if flow is None else flow + part
            return flow

        flow = taken(near_peers, xsend[step, own])
        old = den[0:12, :]
        den[0:12, :] = old - relax_factor * (flow + 0.5 * old + layered[0:12])

        @pl.when(inside)
        def _():
            den[0:12, :] = den[0:12, :] - relax_factor * taken(far_peers, None)

    def cut(i, _):
        at = pl.ds(pl.multiple_of(i * 64, 64), 64)
        whole = operator[at, :]
        high = whole.astype(bf16)
        op1[at, :] = high
        op2[at, :] = (whole - high.astype(f32)).astype(bf16)
        return 0

    def choose():
        hot_row = lax.broadcasted_iota(jnp.int32, (16, 128), 0)
        hot_col = lax.broadcasted_iota(jnp.int32, (16, 128), 1)
        row_item, row_part = lax.bitwise_and(hot_row, 3), lax.shift_right_logical(hot_row, 2)
        col = hot_col - jnp.where(hot_col >= 24, 24, 0) - jnp.where(hot_col >= 48, 24, 0)
        col_pair = lax.shift_right_logical(col * 43, 7)
        col_part = col - 3 * col_pair
        wanted = jnp.full((16, 128), -1, jnp.int32)
        for c in range(OWN):
            for w in range(NW):
                wanted = jnp.where(col_pair == c * NW + w, near[w, c] - first, wanted)
        fits = (row_part == col_part) & (hot_col < 72)
        for g in range(SLOTS):
            hit = fits & (row_item + g * OWN == wanted)
            onehot[pl.ds(g * 16, 16), :] = jnp.where(hit, 1.0, 0.0).astype(bf16)

    pl.semaphore_wait(
        barrier, jnp.where(inside, len(near_peers) + len(far_peers), len(near_peers))
    )
    walls.start()
    load_stiffness.wait()
    send_cells(0)
    itself((0, 1))
    walls.relay(1, 3)
    itself((2, 3))
    walls.relay(2)
    send_density(0)
    choose()
    cell_messages[0].relay(1, 3)
    load_operator.wait()
    lax.fori_loop(0, N // 64, cut, 0)
    cell_messages[0].relay(2)
    layered = operate()
    walls.arrived()

    for step in range(STEPS):
        cells, dens = cell_messages[step], den_messages[step]
        if step == 0:
            by_halves(reverse, lambda: dens.relay(1, 3))
            dens.relay(2)
            send_pieces(step)
        else:
            itself((0, 1, 2, 3))
            cells.relay(1, 3)
            layered = operate()
            cells.relay(2)
            by_halves(reverse, lambda: dens.relay(1, 3))
            dens.relay(2)
            send_pieces(step)
        cells.arrived()
        by_halves(functools.partial(listed, step), lambda: None)
        dens.arrived()
        by_halves(functools.partial(from_walls, step), lambda: None)
        move()
        if step + 1 < STEPS:
            send_cells(step + 1)
        update_density(step, layered)
        if step + 1 < STEPS:
            send_density(step + 1)

    walls.sent()
    for step in range(STEPS):
        cell_messages[step].sent()
        den_messages[step].sent()
        for k in range(7):
            x_copy(step, own, own, (partner, z), k).wait_send()

        @pl.when(inside)
        def _():
            for k in range(7, 11):
                x_copy(step, own, own, (partner, z), k).wait_send()

    for k in range(3):
        at = pl.ds(4 * k, 4)
        out[0, k] = pos[at, :]
        out[1, k] = vel[at, :]
        out[2, k] = den[at, :]


def part_results(state, pos_out, vel_out, den_out):
    for k, ref in enumerate((pos_out, vel_out, den_out)):
        ref[...] = state[k]


def body(
    positions,
    rest_shape,
    modulus,
    stiffness,
    wall_points,
    density,
    wall_operator,
    seg_count,
    neighbours,
    near_patches,
):
    nseg = lax.axis_size("seg")
    vmem = pl.BlockSpec(memory_space=pltpu.VMEM)
    smem = pl.BlockSpec(memory_space=pltpu.SMEM)
    hbm = pl.BlockSpec(memory_space=pl.ANY)
    shape = jax.ShapeDtypeStruct((3, OWN, N), f32)
    dma = pltpu.SemaphoreType.DMA

    def turn(array):
        return jnp.transpose(array, (1, 0, 2))

    state = pl.pallas_call(
        functools.partial(fused, nseg),
        out_shape=jax.ShapeDtypeStruct((3, 3, OWN, N), f32),
        in_specs=[vmem, vmem, smem, hbm, vmem, vmem, hbm, smem, smem, smem],
        out_specs=vmem,
        scratch_shapes=[
            pltpu.VMEM((SLOTS, 12, N), f32),
            pltpu.VMEM((SLOTS, 24, N), f32),
            pltpu.VMEM((SLOTS, 24, N), f32),
            pltpu.VMEM((SLOTS, 12, N), f32),
            pltpu.VMEM((SLOTS, 12, N), f32),
            pltpu.VMEM((STEPS, SLOTS, 12, N), f32),
            pltpu.VMEM((STEPS, SLOTS, 12, N), f32),
            pltpu.VMEM((PAIRS, N, N), bf16),
            pltpu.VMEM((6, N, N), bf16),
            pltpu.VMEM((OWN, 48, N), bf16),
            pltpu.VMEM((OWN, 48, N), bf16),
            pltpu.VMEM((OWN, 16, N), f32),
            pltpu.VMEM((16, N), f32),
            pltpu.VMEM((16, N), f32),
            pltpu.VMEM((16, N), f32),
            pltpu.VMEM((16, N), f32),
            pltpu.VMEM((16, N), f32),
            pltpu.VMEM((3 * PAIRS, N), f32),
            pltpu.VMEM((SLOTS * 16, 128), bf16),
            pltpu.VMEM((N, N), bf16),
            pltpu.VMEM((N, N), bf16),
            dma((5, 11)),
            dma((5, SLOTS)),
            dma((STEPS, 11)),
            dma((STEPS, SLOTS)),
            pltpu.VMEM((N, N), bf16),
            pltpu.VMEM((N, N), f32),
            dma((2,)),
        ],
        compiler_params=pltpu.CompilerParams(collective_id=0, has_side_effects=True),
        name="red_cell_steps",
    )(
        turn(positions),
        turn(rest_shape),
        modulus,
        stiffness,
        turn(wall_points),
        turn(density),
        wall_operator,
        seg_count,
        neighbours,
        near_patches.T,
    )
    outs = pl.pallas_call(
        part_results,
        out_shape=(shape, shape, shape),
        in_specs=[vmem],
        out_specs=(vmem, vmem, vmem),
        name="part_results",
    )(state)
    return tuple(turn(out) for out in outs)


def solution(mesh):
    placed = (
        P(("seg", "cell"), None, None),
        P(("seg", "cell"), None, None),
        P(("seg", "cell")),
        P(),
        P(("seg", "cell"), None, None),
        P(("seg", "cell"), None, None),
        P(),
        P("seg"),
        P(("seg", "cell"), None),
        P(("seg", "cell"), None),
    )
    return jax.shard_map(
        body,
        mesh=mesh,
        in_specs=placed,
        out_specs=(
            P(("seg", "cell"), None, None),
            P(("seg", "cell"), None, None),
            P(("seg", "cell"), None, None),
        ),
        check_vma=False,
    )
```

```python
import functools

import jax
import jax.numpy as jnp
from jax import lax
from jax.experimental import pallas as pl
from jax.experimental.pallas import tpu as pltpu
from jax.sharding import PartitionSpec as P

N = 512
OWN = 4
NZ = 4
NB = 4
NW = 2
STEPS = 2
SLOTS = 3 * NZ
PAIRS = OWN * NW

soften_square = 0.25
stokes_factor = 0.039788735772973836
relax_factor = 0.5
time_step = 0.5

f32, bf16 = jnp.float32, jnp.bfloat16
MESH = pl.DeviceIdType.MESH


def split3(v):
    a = v.astype(bf16).astype(f32)
    r = v - a
    b = r.astype(bf16).astype(f32)
    return a, b, r - b


def rows8(rows):
    rows = list(rows) + [jnp.zeros_like(rows[0])] * (8 - len(rows))
    return jnp.concatenate(rows, 0)


def dot3(a, b):
    return a[0] * b[0] + a[1] * b[1] + a[2] * b[2]


def source_factor(y):
    p = dot3(y, y)
    a, b, c = split3(rows8([-2.0 * y[0], -2.0 * y[1], -2.0 * y[2], jnp.ones_like(p), p]))
    return jnp.concatenate([a, a, b, a, b, c], 0).astype(bf16)


def target_factor(x):
    q = dot3(x, x) + soften_square
    a, b, c = split3(rows8([x[0], x[1], x[2], q, jnp.ones_like(q)]))
    return jnp.concatenate([a, b, a, c, b, a], 0).astype(bf16)


def moments(y, f):
    p, g = dot3(y, y), dot3(y, f)
    one = rows8([f[0], f[1], f[2], g] + [p * f[k] + g * y[k] for k in range(3)] + [f[0] * y[0]])
    two = rows8([f[l] * y[k] for l in range(3) for k in range(3)][1:])
    a, b, _ = split3(jnp.concatenate([one, two], 0))
    return jnp.concatenate([a, b], 0).astype(bf16)


def fold(sums):
    total = sums[0:16] + sums[16:32]
    return total + sums[32:48] if sums.shape[0] == 48 else total


def combine(sums, x):
    row = [sums[k : k + 1] for k in range(16)]
    q = dot3(x, x) + soften_square
    m, g, h = row[0:3], row[3], row[4:7]
    t = [row[7 + 3 * l : 10 + 3 * l] for l in range(3)]
    along = dot3(x, m) - g
    return [
        stokes_factor
        * (
            q * m[k]
            - 2.0 * dot3(x, t[k])
            + h[k]
            + x[k] * along
            - (x[0] * t[0][k] + x[1] * t[1][k] + x[2] * t[2][k])
        )
        for k in range(3)
    ]


def kernel_tile(squares):
    inverse = lax.rsqrt(squares)
    return (inverse * inverse * inverse).astype(bf16)


def mm(a, b):
    return jnp.dot(a, b, preferred_element_type=f32)


def mt(a, b):
    return lax.dot_general(a, b, (((1,), (1,)), ((), ())), preferred_element_type=f32)


def fused(
    nseg,
    pos_in,
    rest_in,
    modulus,
    stiffness_in,
    points_in,
    density_in,
    operator_in,
    seg_count,
    neighbours,
    near,
    out,
    wall,
    cells_first,
    cells_second,
    den_first,
    den_second,
    xsend,
    xrecv,
    pmat,
    pbuf,
    gcell,
    bcell,
    acc,
    pos,
    rest,
    force,
    den,
    vel,
    pieces,
    onehot,
    op1,
    op2,
    send_sem,
    recv_sem,
    x_send,
    x_recv,
    stiffness,
    operator,
    load_sem,
):
    load_stiffness = pltpu.make_async_copy(stiffness_in, stiffness, load_sem.at[0])
    load_operator = pltpu.make_async_copy(operator_in, operator, load_sem.at[1])
    load_stiffness.start()
    load_operator.start()
    seg = lax.axis_index("seg")
    z = lax.axis_index("cell")
    odd = seg % 2
    partner = seg + 1 - 2 * odd
    own = NZ + z

    def turned(d):
        return (z + d) % NZ

    beside = seg + 2 * odd - 1
    inside = (beside >= 0) & (beside < nseg)
    across = (beside + nseg) % nseg
    toward = 1 - 2 * odd

    same = [(seg, 0, d) for d in (1, 2, 3)]
    near_peers = same + [(partner, toward, d) for d in range(NZ)]
    far_peers = [(across, -toward, d) for d in range(NZ)]

    barrier = pltpu.get_barrier_semaphore()

    def greet(peers):
        for segment, _, d in peers:
            pl.semaphore_signal(
                barrier, inc=1, device_id=(segment, turned(d)), device_id_type=MESH
            )

    @pl.when(inside)
    def _():
        greet(far_peers)

    greet(near_peers)

    for ref in (pos, rest, force, den, vel):
        ref[...] = jnp.zeros_like(ref)
    for k in range(3):
        at = pl.ds(4 * k, 4)
        pos[at, :] = pos_in[k]
        rest[at, :] = rest_in[k]
        den[at, :] = density_in[k]
        wall[own, at, :] = points_in[k]

    item16 = lax.bitwise_and(lax.broadcasted_iota(jnp.int32, (16, N), 0), 3)
    alive = jnp.zeros((16, N), f32)
    scale = jnp.zeros((16, N), f32)
    for c in range(OWN):
        one = jnp.where(z * OWN + c < seg_count[0], 1.0, 0.0).astype(f32)
        alive = jnp.where(item16 == c, one, alive)
        scale = jnp.where(item16 == c, one * modulus[c], scale)

    class Message:
        def __init__(self, buffer, number):
            self.buffer, self.number = buffer, number

        def copy(self, source, target, device, k):
            return pltpu.make_async_remote_copy(
                src_ref=self.buffer.at[source],
                dst_ref=self.buffer.at[target],
                send_sem=send_sem.at[self.number, k],
                recv_sem=recv_sem.at[self.number, target],
                device_id=device,
                device_id_type=MESH,
            )

        def start(self):
            for k, d in enumerate((1, 3, 2)):
                self.copy(own, own, (seg, turned(d)), k).start()

            @pl.when(inside)
            def _():
                self.copy(own, 8 - 8 * odd + z, (across, z), 4).start()

            self.copy(own, 8 * odd + z, (partner, z), 3).start()

        def relay(self, *which):
            for d in which:
                slot = NZ + turned(d)
                self.copy(slot, slot, (seg, turned(d)), 0).wait_recv()
                self.hand_on(slot, d)

        def hand_on(self, slot, d):
            @pl.when(inside)
            def _():
                self.copy(slot, 8 - 8 * odd + turned(d), (across, z), 3 + 2 * d).start()

            self.copy(slot, 8 * odd + turned(d), (partner, z), 4 + 2 * d).start()

        def arrived(self):
            for d in range(NZ):
                slot = 8 - 8 * odd + turned(d)
                self.copy(slot, slot, (partner, z), 0).wait_recv()

            @pl.when(inside)
            def _():
                for d in range(NZ):
                    slot = 8 * odd + turned(d)
                    self.copy(slot, slot, (partner, z), 0).wait_recv()

        def sent(self):
            for k in (0, 1, 2, 3, 6, 8, 10):
                self.copy(own, own, (partner, z), k).wait_send()

            @pl.when(inside)
            def _():
                for k in (4, 5, 7, 9):
                    self.copy(own, own, (partner, z), k).wait_send()

    walls = Message(wall, 0)
    cell_messages = [Message(cells_first, 1), Message(cells_second, 2)]
    den_messages = [Message(den_first, 3), Message(den_second, 4)]
    first = (seg - 1) * OWN * NZ

    def rows_of(ref, item):
        return [ref[pl.ds(4 * k + item, 1), :] for k in range(3)]

    def rows_at(ref, slot, item, base=0):
        return [ref[slot, pl.ds(base + 4 * k + item, 1), :] for k in range(3)]

    def place(number):
        relative = jnp.clip(number - first, 0, SLOTS * OWN - 1)
        return lax.shift_right_logical(relative, 2), lax.bitwise_and(relative, 3)

    def tiles(source, target, ref, index):
        for k in range(4):
            ref[index, pl.ds(k * 128, 128), :] = kernel_tile(
                mm(source[k * 128 : (k + 1) * 128], target)
            )

    def make_forces():
        offset = (pos[...] - rest[...]).astype(bf16)
        force[...] = mt(offset, stiffness[...]) * scale

    def send_cells(step):
        make_forces()
        buffer = cell_messages[step].buffer
        buffer[own, 0:12, :] = pos[0:12, :]
        buffer[own, 12:24, :] = force[0:12, :]
        cell_messages[step].start()

    def send_density(step):
        den_messages[step].buffer[own] = den[0:12, :]
        den_messages[step].start()

    def itself(cells):
        for c in cells:
            x, f = rows_of(pos, c), rows_of(force, c)
            g, b = moments(x, f), target_factor(x)
            gcell[c] = g
            bcell[c] = b
            tiles(source_factor(x).T, b, pbuf, c)
            acc[c] = fold(mm(g, pbuf[c]))

    def by_halves(work, between):
        work(0)
        between()
        work(2)

    def reverse(cell):
        for i in range(2):
            for w in range(NW):
                c = cell + i
                slot, item = place(near[w, c])
                y = rows_at(wall, slot, item)
                pair = c * NW + w
                tiles(source_factor(y).T, bcell[c], pmat, pair)
                out = combine(fold(mt(gcell[c], pmat[pair])), y)
                for k in range(3):
                    pieces[pl.ds(3 * pair + k, 1), :] = out[k]

    def listed(step, cell):
        ref = cell_messages[step].buffer
        for i in range(2):
            c = cell + i
            b = bcell[c]
            sums = None
            for n in range(1, NB):
                slot, item = place(neighbours[c, n])
                y, f = rows_at(ref, slot, item), rows_at(ref, slot, item, 12)
                buffer = i * 3 + n - 1
                tiles(source_factor(y).T, b, pbuf, buffer)
                part = mm(moments(y, f), pbuf[buffer])
                sums = part if sums is None else sums + part
            acc[c] = acc[c] + fold(sums)

    def from_walls(step, cell):
        for i in range(2):
            c = cell + i
            sums = None
            for w in range(NW):
                slot, item = place(near[w, c])
                y, f = rows_at(wall, slot, item), rows_at(den_messages[step].buffer, slot, item)
                part = mm(moments(y, f), pmat[c * NW + w])
                sums = part if sums is None else sums + part
            out = combine(acc[c] + fold(sums), rows_of(pos, c))
            for k in range(3):
                vel[pl.ds(4 * k + c, 1), :] = out[k]

    def x_copy(step, group, target, device, k):
        return pltpu.make_async_remote_copy(
            src_ref=xsend.at[step, group],
            dst_ref=xrecv.at[step, target],
            send_sem=x_send.at[step, k],
            recv_sem=x_recv.at[step, target],
            device_id=device,
            device_id_type=MESH,
        )

    def send_pieces(step):
        high, middle, low = split3(pieces[...])
        spread = jnp.concatenate([high, middle, low, jnp.zeros((56, N), f32)], 0).astype(bf16)
        shares = mm(onehot[...], spread)
        for g in range(SLOTS):
            xsend[step, g] = shares[g * 16 : g * 16 + 12]
        @pl.when(inside)
        def _():
            start_shares(step, far_peers, 7)

        start_shares(step, near_peers, 0)

    def start_shares(step, peers, base):
        for k, (segment, away, d) in enumerate(peers):
            x_copy(
                step,
                (away + 1) * NZ + turned(d),
                (1 - away) * NZ + z,
                (segment, turned(d)),
                base + k,
            ).start()

    def operate():
        high, middle, low = split3(den[...])
        layered = fold(mt(jnp.concatenate([high, middle, low], 0).astype(bf16), op1[...]))
        second = mt(jnp.concatenate([high, middle], 0).astype(bf16), op2[...])
        return layered + second[0:16] + second[16:32]

    def move():
        speed = alive * vel[...]
        vel[...] = speed
        pos[...] = pos[...] + time_step * speed

    def update_density(step, layered):
        def taken(peers, flow):
            for _, away, d in peers:
                slot = (1 + away) * NZ + turned(d)
                x_copy(step, own, slot, (partner, z), 0).wait_recv()
                part = xrecv[step, slot]
                flow = part if flow is None else flow + part
            return flow

        flow = taken(near_peers, xsend[step, own])
        old = den[0:12, :]
        den[0:12, :] = old - relax_factor * (flow + 0.5 * old + layered[0:12])

        @pl.when(inside)
        def _():
            den[0:12, :] = den[0:12, :] - relax_factor * taken(far_peers, None)

    def cut(i, _):
        at = pl.ds(pl.multiple_of(i * 64, 64), 64)
        whole = operator[at, :]
        high = whole.astype(bf16)
        op1[at, :] = high
        op2[at, :] = (whole - high.astype(f32)).astype(bf16)
        return 0

    def choose():
        hot_row = lax.broadcasted_iota(jnp.int32, (16, 128), 0)
        hot_col = lax.broadcasted_iota(jnp.int32, (16, 128), 1)
        row_item, row_part = lax.bitwise_and(hot_row, 3), lax.shift_right_logical(hot_row, 2)
        col = hot_col - jnp.where(hot_col >= 24, 24, 0) - jnp.where(hot_col >= 48, 24, 0)
        col_pair = lax.shift_right_logical(col * 43, 7)
        col_part = col - 3 * col_pair
        wanted = jnp.full((16, 128), -1, jnp.int32)
        for c in range(OWN):
            for w in range(NW):
                wanted = jnp.where(col_pair == c * NW + w, near[w, c] - first, wanted)
        fits = (row_part == col_part) & (hot_col < 72)
        for g in range(SLOTS):
            hit = fits & (row_item + g * OWN == wanted)
            onehot[pl.ds(g * 16, 16), :] = jnp.where(hit, 1.0, 0.0).astype(bf16)

    pl.semaphore_wait(
        barrier, jnp.where(inside, len(near_peers) + len(far_peers), len(near_peers))
    )
    walls.start()
    load_stiffness.wait()
    send_cells(0)
    itself((0, 1))
    walls.relay(1, 3)
    itself((2, 3))
    walls.relay(2)
    send_density(0)
    choose()
    cell_messages[0].relay(1, 3)
    load_operator.wait()
    lax.fori_loop(0, N // 64, cut, 0)
    cell_messages[0].relay(2)
    layered = operate()
    walls.arrived()

    for step in range(STEPS):
        cells, dens = cell_messages[step], den_messages[step]
        if step == 0:
            by_halves(reverse, lambda: dens.relay(1, 3))
            dens.relay(2)
            send_pieces(step)
        else:
            itself((0, 1, 2, 3))
            cells.relay(1, 3)
            layered = operate()
            cells.relay(2)
            by_halves(reverse, lambda: dens.relay(1, 3))
            dens.relay(2)
            send_pieces(step)
        cells.arrived()
        by_halves(functools.partial(listed, step), lambda: None)
        dens.arrived()
        by_halves(functools.partial(from_walls, step), lambda: None)
        move()
        if step + 1 < STEPS:
            send_cells(step + 1)
        update_density(step, layered)
        if step + 1 < STEPS:
            send_density(step + 1)

    walls.sent()
    for step in range(STEPS):
        cell_messages[step].sent()
        den_messages[step].sent()
        for k in range(7):
            x_copy(step, own, own, (partner, z), k).wait_send()

        @pl.when(inside)
        def _():
            for k in range(7, 11):
                x_copy(step, own, own, (partner, z), k).wait_send()

    for k in range(3):
        at = pl.ds(4 * k, 4)
        out[0, k] = pos[at, :]
        out[1, k] = vel[at, :]
        out[2, k] = den[at, :]


def part_results(state, pos_out, vel_out, den_out):
    for k, ref in enumerate((pos_out, vel_out, den_out)):
        ref[...] = state[k]


def body(
    positions,
    rest_shape,
    modulus,
    stiffness,
    wall_points,
    density,
    wall_operator,
    seg_count,
    neighbours,
    near_patches,
):
    nseg = lax.axis_size("seg")
    vmem = pl.BlockSpec(memory_space=pltpu.VMEM)
    smem = pl.BlockSpec(memory_space=pltpu.SMEM)
    hbm = pl.BlockSpec(memory_space=pl.ANY)
    shape = jax.ShapeDtypeStruct((3, OWN, N), f32)
    dma = pltpu.SemaphoreType.DMA

    def turn(array):
        return jnp.transpose(array, (1, 0, 2))

    state = pl.pallas_call(
        functools.partial(fused, nseg),
        out_shape=jax.ShapeDtypeStruct((3, 3, OWN, N), f32),
        in_specs=[vmem, vmem, smem, hbm, vmem, vmem, hbm, smem, smem, smem],
        out_specs=vmem,
        scratch_shapes=[
            pltpu.VMEM((SLOTS, 12, N), f32),
            pltpu.VMEM((SLOTS, 24, N), f32),
            pltpu.VMEM((SLOTS, 24, N), f32),
            pltpu.VMEM((SLOTS, 12, N), f32),
            pltpu.VMEM((SLOTS, 12, N), f32),
            pltpu.VMEM((STEPS, SLOTS, 12, N), f32),
            pltpu.VMEM((STEPS, SLOTS, 12, N), f32),
            pltpu.VMEM((PAIRS, N, N), bf16),
            pltpu.VMEM((6, N, N), bf16),
            pltpu.VMEM((OWN, 32, N), bf16),
            pltpu.VMEM((OWN, 48, N), bf16),
            pltpu.VMEM((OWN, 16, N), f32),
            pltpu.VMEM((16, N), f32),
            pltpu.VMEM((16, N), f32),
            pltpu.VMEM((16, N), f32),
            pltpu.VMEM((16, N), f32),
            pltpu.VMEM((16, N), f32),
            pltpu.VMEM((3 * PAIRS, N), f32),
            pltpu.VMEM((SLOTS * 16, 128), bf16),
            pltpu.VMEM((N, N), bf16),
            pltpu.VMEM((N, N), bf16),
            dma((5, 11)),
            dma((5, SLOTS)),
            dma((STEPS, 11)),
            dma((STEPS, SLOTS)),
            pltpu.VMEM((N, N), bf16),
            pltpu.VMEM((N, N), f32),
            dma((2,)),
        ],
        compiler_params=pltpu.CompilerParams(collective_id=0, has_side_effects=True),
        name="red_cell_steps",
    )(
        turn(positions),
        turn(rest_shape),
        modulus,
        stiffness,
        turn(wall_points),
        turn(density),
        wall_operator,
        seg_count,
        neighbours,
        near_patches.T,
    )
    outs = pl.pallas_call(
        part_results,
        out_shape=(shape, shape, shape),
        in_specs=[vmem],
        out_specs=(vmem, vmem, vmem),
        name="part_results",
    )(state)
    return tuple(turn(out) for out in outs)


def solution(mesh):
    placed = (
        P(("seg", "cell"), None, None),
        P(("seg", "cell"), None, None),
        P(("seg", "cell")),
        P(),
        P(("seg", "cell"), None, None),
        P(("seg", "cell"), None, None),
        P(),
        P("seg"),
        P(("seg", "cell"), None),
        P(("seg", "cell"), None),
    )
    return jax.shard_map(
        body,
        mesh=mesh,
        in_specs=placed,
        out_specs=(
            P(("seg", "cell"), None, None),
            P(("seg", "cell"), None, None),
            P(("seg", "cell"), None, None),
        ),
        check_vma=False,
    )
```
